128 devices in a mesh: row: 16 (over x, y_lo, core), col: 8 (over z, y_hi).
Axes of the slice: x: 4, y: 4 (y_hi: 2, y_lo: 2; y = y_hi * 2 + y_lo), z: 4, core: 2. Of those that a mesh axis runs over, the one named last changes fastest.
Arguments:
- documents: bfloat16 [2, 16384, 2048], P(None, ('row', 'col')), may hold values from -6 to 6
- targets: bfloat16 [2, 16384, 2048], P(None, ('row', 'col')), may hold values from -6 to 6
- routes: int32 [2, 16384, 1], P(None, ('row', 'col')), may hold values from 0 to 127; in each aligned block of 128 rows (0 to 127, 128 to 255, ..., all dimensions but the last counted through in order) at most 2 rows name the same one
- doc_counts: int32 [16, 8], replicated, may hold values from 1 to 64
- module_one: float32 [16, 2048, 2048], P('row', 'col'), may hold values from -6 to 6
- module_two: float32 [8, 2048, 2048], P('col', 'row'), may hold values from -6 to 6
- moment_one: float32 [16, 2048, 2048], P('row', 'col'), may hold values from -0.75 to 0.75
- moment_two: float32 [8, 2048, 2048], P('col', 'row'), may hold values from -0.75 to 0.75
Outputs:
- new_one: float32 [16, 2048, 2048], P('row', 'col')
- new_two: float32 [8, 2048, 2048], P('col', 'row')
- next_moment_one: float32 [16, 2048, 2048], P('row', 'col')
- next_moment_two: float32 [8, 2048, 2048], P('col', 'row')
The draws below stay inside these ranges and needn't reach their ends.
Inputs may be any that keep to these rules, and one draw needn't show every extreme that they name: `routes`: in each micro-batch, at most 2 of the 128 rows that one device holds name the same path.
All inputs are finite; a program needn't handle non-finite values.
Results may differ from the reference program's by a relative error of at most 0.011.
Values may be sent and summed in bfloat16 or wider, within the bound.
A program may use at most 192 MiB of HBM per device.

```python
import math
import jax
import jax.numpy as jnp
import numpy as np
from jax import lax

D = 2048
ROWS_DEV = 128
MICRO = 2
PATHS = 128
CAP = 2
TOKENS = 16384
N_ROW = 16
N_COL = 8


def place_ends(drawn, rng, smallest, largest):
    spot = [jax.random.randint(jax.random.fold_in(rng, axis), (), 0, length) for axis, length in enumerate(drawn.shape)]
    widest = drawn.shape.index(max(drawn.shape))
    next_to = spot[:widest] + [(spot[widest] + 1) % drawn.shape[widest]] + spot[widest + 1:]
    return drawn.at[tuple(spot)].set(smallest).at[tuple(next_to)].set(largest)


def level_of(key, dims, split, smallest, top_value):
    factor_of, own = 1.0, jax.random.fold_in(key, 6)
    for dim, parts in split:
        heights = jnp.exp(jax.random.uniform(jax.random.fold_in(own, dim), (parts,), jnp.float32, smallest / len(split), top_value / len(split)))
        factor_of = factor_of * jnp.repeat(heights, dims[dim] // parts).reshape([-1 if axis == dim else 1 for axis in range(len(dims))])
    return factor_of


def shared_out(stream_key, own, number, rows, amount, top, bound, slope):
    order = jax.random.permutation(stream_key, amount)
    crowded, ordinary = load_shares(amount, rows * top, bound, slope, True), load_shares(amount, rows * top, bound, slope, False)
    places = jnp.arange(amount)

    def named(lengths, offset_by):
        used = int((lengths > 0).sum())
        fixed = max(1, used // 4)
        moved = fixed + (places - fixed + offset_by * (used - fixed)) % max(1, amount - fixed)
        return jnp.zeros((amount,), jnp.int32).at[order[jnp.where(places < fixed, places, moved)]].set(jnp.asarray(lengths, jnp.int32))

    lengths = jnp.where(number % 4 == 0, named(crowded, number // 4), named(ordinary, number - number // 4 - 1))
    mixed = jax.random.permutation(jax.random.fold_in(own, 3), amount)
    source_of, receiver = mixed[0:amount // 2 * 2:2], mixed[1:amount // 2 * 2:2]
    room = jnp.minimum(lengths[source_of] - 1, bound - lengths[receiver]) // 2
    room = jnp.where((source_of == order[0]) | (receiver == order[0]) | (lengths[receiver] == 0), 0, jnp.maximum(room, 0))
    moved = jax.random.randint(jax.random.fold_in(own, 4), (amount // 2,), 0, 1 << 20) % (room + 1)
    lengths = lengths.at[source_of].add(-moved).at[receiver].add(moved)
    labels = jnp.searchsorted(jnp.cumsum(lengths), jnp.arange(rows * top), side="right").astype(jnp.int32)
    grid = labels.reshape(top, rows).T
    grid = grid[jax.random.permutation(jax.random.fold_in(own, 1), rows)]
    offset_by = jax.random.randint(jax.random.fold_in(own, 2), (rows, 1), 0, top)
    return jnp.take_along_axis(grid, (jnp.arange(top)[None, :] + offset_by) % top, axis=1)


def load_shares(number_of, total, limit, lean, full):
    loads = [(1 << 20) // math.isqrt(standing ** lean) + 1 for standing in range(1, number_of + 1)]
    largest = limit if full else min(limit, max(-(-total // number_of), total * loads[0] // sum(loads)))
    least = 1 if total - largest >= number_of - 1 else 0
    holding, rest = [largest] + [least] * (number_of - 1), total - largest - least * (number_of - 1)
    while rest > 0:
        candidates = [i for i in range(1, number_of) if holding[i] < largest] or [i for i in range(1, number_of) if holding[i] < limit]
        whole, left = sum([loads[i] for i in candidates]), rest
        for i in candidates:
            addition = min(limit - holding[i], max(1, left * loads[i] // whole), rest)
            holding[i] = holding[i] + addition
            rest = rest - addition
    return np.array(holding)


def bell_draw(key, shape, scale, reach, shards=(), held_as=jnp.bfloat16):
    drawn = jax.random.normal(key, shape, jnp.float32) * scale
    if len(shards) > 0:
        drawn = level_of(key, shape, shards, -0.22, 0.18) * drawn
    return jnp.clip(drawn, min=-reach, max=reach).astype(held_as)


def setup_inputs(seed: int = 0) -> dict:
    key_list = jax.random.split(jax.random.key(seed), 9)
    documents = bell_draw(key_list[0], (MICRO, TOKENS, D), 1.0, 6.0, ((1, 128),))
    targets = bell_draw(key_list[1], (MICRO, TOKENS, D), 1.0, 6.0, ((1, 128),))
    routes_keys = jax.random.split(jax.random.fold_in(key_list[2], 1), MICRO * TOKENS // ROWS_DEV)
    routes_turns = jax.random.permutation(jax.random.fold_in(key_list[2], 3), MICRO * TOKENS // ROWS_DEV)
    routes = jax.vmap(lambda own, number: shared_out(jax.random.fold_in(key_list[2], 2), own, number, ROWS_DEV, PATHS, 1, CAP, 2))(routes_keys, routes_turns).reshape((MICRO, TOKENS, 1))
    doc_counts = place_ends(jax.random.randint(key_list[3], (N_ROW, N_COL), 1, 65), jax.random.fold_in(key_list[3], 1), 1, 64).astype(jnp.int32)
    module_one = bell_draw(key_list[4], (N_ROW, D, D), 1.0, 6.0, ((0, 16), (1, 8)), jnp.float32)
    module_two = bell_draw(key_list[5], (N_COL, D, D), 1.0, 6.0, ((0, 8), (1, 16)), jnp.float32)
    moment_one = bell_draw(key_list[6], (N_ROW, D, D), 0.05, 0.75, ((0, 16), (1, 8)), jnp.float32)
    moment_two = bell_draw(key_list[7], (N_COL, D, D), 0.05, 0.75, ((0, 8), (1, 16)), jnp.float32)
    return dict(documents=documents, targets=targets, routes=routes, doc_counts=doc_counts, module_one=module_one, module_two=module_two, moment_one=moment_one, moment_two=moment_two)


beta_one = 0.9
beta_two = 0.95
inner_rate = 0.1
decay = 0.1
outer_rate = 0.7
outer_moment = 0.9

def silu_slope(pre):
    sig = jax.nn.sigmoid(pre)
    return sig * (1.0 + pre * (1.0 - sig))

def gradients(w_one, w_two, rows, targs, valid):
    scale = D ** (-0.5)
    pre = jnp.dot(rows, w_one, preferred_element_type=jnp.float32) * scale
    hidden = jax.nn.silu(pre).astype(jnp.bfloat16)
    out = rows.astype(jnp.float32) + jnp.dot(hidden, w_two, preferred_element_type=jnp.float32) * scale
    error = ((out - targs.astype(jnp.float32)) * valid / ROWS_DEV).astype(jnp.bfloat16)
    grad_two = lax.dot_general(hidden, error, (((0,), (0,)), ((), ())), preferred_element_type=jnp.float32) * scale
    back = lax.dot_general(error, w_two, (((1,), (1,)), ((), ())), preferred_element_type=jnp.float32) * scale
    inner = (back * silu_slope(pre)).astype(jnp.bfloat16)
    grad_one = lax.dot_general(rows, inner, (((0,), (0,)), ((), ())), preferred_element_type=jnp.float32) * scale
    return (grad_one, grad_two)

def adamw(param, grad, first, second, step, guard):
    first = beta_one * first + (1.0 - beta_one) * grad
    second = beta_two * second + (1.0 - beta_two) * grad * grad
    fix_one = 1.0 - beta_one ** (step + 1)
    fix_two = 1.0 - beta_two ** (step + 1)
    update = first / fix_one / (jnp.sqrt(second / fix_two) + guard) + decay * param
    return (param - inner_rate * update, first, second)

def train_path(start_one, start_two, documents, targets, routes, path):
    slots = N_ROW * N_COL * CAP
    guard = 0.5 / (D * ROWS_DEV) ** 0.5
    p_one = start_one.astype(jnp.float32)
    p_two = start_two.astype(jnp.float32)
    m_one = jnp.zeros_like(p_one)
    v_one = jnp.zeros_like(p_one)
    m_two = jnp.zeros_like(p_two)
    v_two = jnp.zeros_like(p_two)
    for step in range(MICRO):
        dest = routes[step, :, 0]
        order = jnp.argsort((dest != path).astype(jnp.int32), stable=True)[:slots]
        hit = jnp.take(dest, order) == path
        valid = hit.astype(jnp.float32)[:, None]
        rows = jnp.where(hit[:, None], jnp.take(documents[step], order, axis=0), jnp.zeros((), jnp.bfloat16))
        targs = jnp.where(hit[:, None], jnp.take(targets[step], order, axis=0), jnp.zeros((), jnp.bfloat16))
        grad_one, grad_two = gradients(p_one.astype(jnp.bfloat16), p_two.astype(jnp.bfloat16), rows, targs, valid)
        p_one, m_one, v_one = adamw(p_one, grad_one, m_one, v_one, step, guard)
        p_two, m_two, v_two = adamw(p_two, grad_two, m_two, v_two, step, guard)
    return (start_one.astype(jnp.float32) - p_one, start_two.astype(jnp.float32) - p_two)

def rounded(value):
    return lax.optimization_barrier(value.astype(jnp.bfloat16)).astype(jnp.float32)

def reference(documents, targets, routes, doc_counts, module_one, module_two, moment_one, moment_two):
    counts = doc_counts.astype(jnp.float32)
    weight_one = counts / lax.optimization_barrier(jnp.sum(counts, axis=1, keepdims=True))
    weight_two = counts / lax.optimization_barrier(jnp.sum(counts, axis=0, keepdims=True))
    start_one_all = module_one.astype(jnp.bfloat16)
    start_two_all = module_two.astype(jnp.bfloat16)

    def visit(carry, path):
        sum_one, sum_two = carry
        index_one = (path // N_COL).astype(jnp.int32)
        index_two = (path % N_COL).astype(jnp.int32)
        start_one = lax.dynamic_index_in_dim(start_one_all, index_one, 0, keepdims=False)
        start_two = lax.dynamic_index_in_dim(start_two_all, index_two, 0, keepdims=False)
        delta_one, delta_two = train_path(start_one, start_two, documents, targets, routes, path)
        term_one = rounded(weight_one[index_one, index_two] * delta_one)
        term_two = rounded(weight_two[index_one, index_two] * delta_two)
        sum_one = sum_one.at[index_one].add(term_one)
        sum_two = sum_two.at[index_two].add(term_two)
        return ((sum_one, sum_two), None)
    init = (jnp.zeros(module_one.shape, jnp.float32), jnp.zeros(module_two.shape, jnp.float32))
    (avg_one, avg_two), unused = lax.scan(visit, init, jnp.arange(N_ROW * N_COL, dtype=jnp.int32))
    next_moment_one = outer_moment * moment_one + avg_one
    next_moment_two = outer_moment * moment_two + avg_two
    new_one = module_one - outer_rate * (outer_moment * next_moment_one + avg_one)
    new_two = module_two - outer_rate * (outer_moment * next_moment_two + avg_two)
    return (new_one, new_two, next_moment_one, next_moment_two)
```

```python
import functools

import jax
import jax.numpy as jnp
from jax import lax
from jax.experimental import pallas as pl
from jax.experimental.pallas import tpu as pltpu
from jax.sharding import PartitionSpec as P

D = 2048
ROWS = 128
PATHS = 128
SLOTS = 256
N_ROW = 16
N_COL = 8
SCALE = D ** (-0.5)
GUARD = 0.5 / (D * ROWS) ** 0.5 / SCALE

outer_rate = 0.7
outer_moment = 0.9

BF = jnp.bfloat16
F32 = jnp.float32
MESH = pl.DeviceIdType.MESH
ANY = pl.BlockSpec(memory_space=pl.ANY)
VMEM = pl.BlockSpec(memory_space=pltpu.VMEM)


def iota(shape, dim):
    return lax.broadcasted_iota(jnp.int32, shape, dim)


def pack_kernel(dest_col, dest_row, docs, targs, out):
    block = pl.program_id(0)
    picks = []
    for m in range(2):
        row = dest_row[m : m + 1, :]
        same = jnp.where(dest_col[m] == row, 1, 0)
        earlier = jnp.where(iota((ROWS, ROWS), 0) < iota((ROWS, ROWS), 1), same, 0)
        rank = jnp.sum(earlier, axis=0, keepdims=True)
        for kind in range(2):
            slot = row * 8 + (m * 4 + kind * 2) + rank - block * 128
            picks.append(jnp.where(iota((128, ROWS), 0) == slot, 1.0, 0.0).astype(BF))
    total = jnp.dot(picks[0], docs[0], preferred_element_type=F32)
    total += jnp.dot(picks[1], targs[0], preferred_element_type=F32)
    total += jnp.dot(picks[2], docs[1], preferred_element_type=F32)
    total += jnp.dot(picks[3], targs[1], preferred_element_type=F32)
    out[...] = total.astype(BF)


def pack(routes, docs, targs):
    full = lambda *shape: pl.BlockSpec(shape, lambda i: (0,) * len(shape))
    return pl.pallas_call(
        pack_kernel,
        grid=(8,),
        out_shape=jax.ShapeDtypeStruct((PATHS * 8, D), BF),
        in_specs=[full(2, ROWS, 1), full(2, ROWS), full(2, ROWS, D), full(2, ROWS, D)],
        out_specs=pl.BlockSpec((128, D), lambda i: (i, 0)),
        name="pack",
    )(routes, routes.reshape(2, ROWS), docs, targs)


def places():
    row, col = lax.axis_index("row"), lax.axis_index("col")
    x, low, core = row // 4, (row // 2) % 2, row % 2
    z, high = col // 2, col % 2

    def device(x=x, low=low, core=core, z=z, high=high):
        return (x * 4 + low * 2 + core, z * 2 + high)

    return row, col, x, low, core, z, high, device


def towers():
    row, col, x, low, core, z, high, device = places()
    one = dict(
        place=z,
        size=256,
        partner=device(high=1 - high),
        plus=device(z=(z + 1) % 4),
        minus=device(z=(z + 3) % 4),
        rows=lambda place, j: pl.multiple_of((place * 2 + (high + j) % 2) * 256, 256),
    )
    two = dict(
        place=x,
        size=128,
        partner=device(low=1 - low),
        plus=device(x=(x + 1) % 4),
        minus=device(x=(x + 3) % 4),
        rows=lambda place, j: pl.multiple_of((place * 4 + ((low + j) % 2) * 2 + core) * 128, 128),
    )
    return one, two, device(core=1 - core)


def remote(src, dst, send, recv, device):
    copy = pltpu.make_async_remote_copy(
        src_ref=src, dst_ref=dst, send_sem=send, recv_sem=recv, device_id=device, device_id_type=MESH
    )
    return copy


def gather_kernel(own_one, own_two, slots, w_one, w_two, got, y_sem, ring_sem, fwd_sem, core_sem, local_sem, a2a_sem):
    one, two, twin = towers()
    row, col = lax.axis_index("row"), lax.axis_index("col")
    me = row * N_COL + col
    sent = []

    def start(copy):
        copy.start()
        sent.append(copy)
        return copy

    class Tower:
        pass

    ts = []
    for n, (place, own, full) in enumerate(((one, own_one, w_one), (two, own_two, w_two))):
        t = Tower()
        t.n, t.own, t.full, t.half = n, own, full, place["size"] // 2
        t.__dict__.update(place)
        ts.append(t)

    def part(t, place, j, first, count):
        return t.full.at[pl.ds(t.rows(place, j) + first, count)]

    def spread(t, j):
        half = t.half
        for way, device in ((0, t.plus), (1, t.minus)):
            for which in (0, 1) if way == 0 else (1, 0):
                dst = part(t, t.place, j, which * half, half)
                src = t.own.at[pl.ds(which * half, half)] if j == 0 else dst
                start(remote(src, dst, ring_sem.at[0, t.n, j, way, which], ring_sem.at[1, t.n, j, way, which], device))

    def arrived(t, j, way, which):
        place = (t.place + (3 if way == 0 else 1)) % 4
        ref = part(t, place, j, which * t.half, t.half)
        remote(ref, ref, ring_sem.at[0, t.n, j, way, which], ring_sem.at[1, t.n, j, way, which], t.plus).wait_recv()

    def forward(t, j, way):
        arrived(t, j, way, way)
        place = (t.place + (3 if way == 0 else 1)) % 4
        ref = part(t, place, j, way * t.half, t.half)
        start(remote(ref, ref, fwd_sem.at[0, t.n, j, way], fwd_sem.at[1, t.n, j, way], t.plus if way == 0 else t.minus))

    def forwarded(t, j, way):
        ref = part(t, (t.place + 2) % 4, j, way * t.half, t.half)
        remote(ref, ref, fwd_sem.at[0, t.n, j, way], fwd_sem.at[1, t.n, j, way], t.plus).wait_recv()

    def to_twin(step, j):
        t = ts[1]
        dst = part(t, (t.place + step) % 4, j, 0, 128)
        src = t.own if step == 0 and j == 0 else dst
        start(remote(src, dst, core_sem.at[0, step, j], core_sem.at[1, step, j], twin))

    for t in ts:
        ref = part(t, t.place, 0, 0, 2 * t.half)
        start(remote(t.own, ref, y_sem.at[0, t.n], y_sem.at[1, t.n], t.partner))
        spread(t, 0)
    to_twin(0, 0)
    locals_ = [
        pltpu.make_async_copy(t.own, part(t, t.place, 0, 0, 2 * t.half), local_sem.at[t.n]) for t in ts
    ]
    locals_.append(pltpu.make_async_copy(slots.at[me], got.at[me], local_sem.at[2]))
    for copy in locals_:
        copy.start()

    def send_slots(step, carry):
        peer = (me + step) % PATHS
        remote(slots.at[peer], got.at[me], a2a_sem.at[0], a2a_sem.at[1], (peer // N_COL, peer % N_COL)).start()
        return carry

    lax.fori_loop(1, PATHS, send_slots, 0)
    for t in ts:
        ref = part(t, t.place, 1, 0, 2 * t.half)
        remote(ref, ref, y_sem.at[0, t.n], y_sem.at[1, t.n], t.partner).wait_recv()
        spread(t, 1)
    to_twin(0, 1)
    for j in range(2):
        for t in ts:
            for way in range(2):
                forward(t, j, way)
    for j in range(2):
        for t in ts:
            arrived(t, j, 0, 1)
            arrived(t, j, 1, 0)
        to_twin(1, j)
        to_twin(3, j)
    for j in range(2):
        for t in ts:
            forwarded(t, j, 0)
            forwarded(t, j, 1)
        to_twin(2, j)
    t = ts[1]
    for step in range(4):
        for j in range(2):
            rows = ((t.place + step) % 4 * 4 + ((row // 2 + j) % 2) * 2 + 1 - row % 2) * 128
            ref = t.full.at[pl.ds(pl.multiple_of(rows, 128), 128)]
            remote(ref, ref, core_sem.at[0, step, j], core_sem.at[1, step, j], twin).wait_recv()
    for copy in locals_:
        copy.wait()
    for copy in sent:
        copy.wait_send()
    all_slots = remote(
        slots.at[pl.ds(0, PATHS - 1)], got.at[pl.ds(0, PATHS - 1)], a2a_sem.at[0], a2a_sem.at[1], twin
    )
    all_slots.wait_send()
    all_slots.wait_recv()


def gather(own_one, own_two, slots):
    sem = pltpu.SemaphoreType.DMA
    return pl.pallas_call(
        gather_kernel,
        out_shape=(
            jax.ShapeDtypeStruct((D, D), BF),
            jax.ShapeDtypeStruct((D, D), BF),
            jax.ShapeDtypeStruct((PATHS, 8, D), BF),
        ),
        in_specs=[VMEM] * 3,
        out_specs=(ANY,) * 3,
        scratch_shapes=[
            sem((2, 2)),
            sem((2, 2, 2, 2, 2)),
            sem((2, 2, 2, 2)),
            sem((2, 4, 2)),
            sem((3,)),
            sem((2,)),
        ],
        compiler_params=pltpu.CompilerParams(has_side_effects=True),
        name="gather",
    )(own_one, own_two, slots)


def compute_kernel(
    share, got, w_one, w_two, t_one, t_two, one, two, g_one, g_two, x, y, hid, err, inn, slope, x_t, h_t, sem
):
    loads = [pltpu.make_async_copy(w_one, one, sem.at[0]), pltpu.make_async_copy(w_two, two, sem.at[1])]
    for copy in loads:
        copy.start()
    o, i = iota((256, 256), 0), iota((256, 256), 1)
    pick = jnp.where(i == (o % 64) // 2 * 8 + o // 64 * 2 + o % 2, 1.0, 0.0).astype(BF)
    for b in range(4):
        rows = jnp.dot(pick, got[b * 256 : (b + 1) * 256, :], preferred_element_type=F32).astype(BF)
        for m in range(2):
            x[m, b * 64 : (b + 1) * 64, :] = rows[m * 128 : m * 128 + 64]
            y[m, b * 64 : (b + 1) * 64, :] = rows[m * 128 + 64 : m * 128 + 128]

    tile = 256

    def spans(n):
        return pl.ds(pl.multiple_of(n * tile, tile), tile)

    def passes(m, first):
        def pre_tile(n, carry):
            cols = spans(n)
            pre = jnp.dot(x[m], one[:, cols], preferred_element_type=F32) * SCALE
            sig = 1.0 / (1.0 + jnp.exp(-pre))
            hidden = (pre * sig).astype(BF)
            hid[:, cols] = hidden
            h_t[cols, :] = hidden.T
            slope[:, cols] = sig * (1.0 + pre * (1.0 - sig))
            x_t[cols, :] = x[m, :, cols].T
            return carry

        if first:
            loads[0].wait()
        lax.fori_loop(0, D // tile, pre_tile, 0)
        if first:
            loads[1].wait()

        def err_tile(n, carry):
            cols = spans(n)
            out = jnp.dot(hid[...], two[:, cols], preferred_element_type=F32) * SCALE
            out = x[m, :, cols].astype(F32) + out
            err[:, cols] = ((out - y[m, :, cols].astype(F32)) / ROWS).astype(BF)
            return carry

        lax.fori_loop(0, D // tile, err_tile, 0)

        def inn_tile(n, carry):
            cols = spans(n)
            back = lax.dot_general(err[...], two[cols, :], (((1,), (1,)), ((), ())), preferred_element_type=F32)
            inn[:, cols] = (back * SCALE * slope[:, cols]).astype(BF)
            return carry

        lax.fori_loop(0, D // tile, inn_tile, 0)

    def first_update(left, right, w, g):
        def step(n, carry):
            rows, cols = spans(n // 4), pl.ds(pl.multiple_of(n % 4 * 512, 512), 512)
            grad = jnp.dot(left[rows, :], right[:, cols], preferred_element_type=F32)
            update = grad / (jnp.abs(grad) + GUARD)
            g[rows, cols] = grad.astype(BF)
            w[rows, cols] = (0.99 * w[rows, cols].astype(F32) - 0.1 * update).astype(BF)
            return carry

        lax.fori_loop(0, 32, step, 0)

    def last_update(left, right, w, g, weight):
        part_w, part_a, part_b = weight * (1.0 / 0.99 - 0.99), weight * (0.1 / 0.99), weight * 0.1

        def step(n, carry):
            rows, cols = spans(n // 4), pl.ds(pl.multiple_of(n % 4 * 512, 512), 512)
            grad = jnp.dot(left[rows, :], right[:, cols], preferred_element_type=F32)
            before = g[rows, cols].astype(F32)
            update_a = before / (jnp.abs(before) + GUARD)
            first = (0.09 / 0.19) * before + (0.1 / 0.19) * grad
            second = (0.0475 / 0.0975) * (before * before) + (0.05 / 0.0975) * (grad * grad)
            update_b = first / (jnp.sqrt(second) + GUARD)
            g[rows, cols] = (
                part_w * w[rows, cols].astype(F32) + part_a * update_a + part_b * update_b
            ).astype(BF)
            return carry

        lax.fori_loop(0, 32, step, 0)

    passes(0, True)
    first_update(h_t, err, two, g_two)
    first_update(x_t, inn, one, g_one)
    passes(1, False)
    last_update(x_t, inn, one, g_one, share[0])
    out_one = pltpu.make_async_copy(g_one, t_one, sem.at[0])
    out_one.start()
    last_update(h_t, err, two, g_two, share[1])
    out_two = pltpu.make_async_copy(g_two, t_two, sem.at[1])
    out_two.start()
    out_one.wait()
    out_two.wait()


def compute(share, got, w_one, w_two):
    square = jax.ShapeDtypeStruct((D, D), BF)
    act = pltpu.VMEM((SLOTS, D), BF)
    return pl.pallas_call(
        compute_kernel,
        out_shape=(square, square),
        in_specs=[pl.BlockSpec(memory_space=pltpu.SMEM), VMEM, ANY, ANY],
        out_specs=(ANY, ANY),
        scratch_shapes=[pltpu.VMEM((D, D), BF)] * 4
        + [pltpu.VMEM((2, SLOTS, D), BF)] * 2
        + [act] * 3
        + [pltpu.VMEM((SLOTS, D), F32)]
        + [pltpu.VMEM((D, SLOTS), BF)] * 2
        + [pltpu.SemaphoreType.DMA((2,))],
        compiler_params=pltpu.CompilerParams(vmem_limit_bytes=60 * 2**20),
        name="compute",
    )(share, got, w_one, w_two)


def reduce_kernel(
    t_one, t_two, avg_one, avg_two,
    early_one, early_two, late_one, late_two, pair_one, pair_two, core_in, core_sum, y_out_one, y_out_two,
    early_sem, late_sem, y_sem, core_sem,
):
    one, two, twin = towers()
    row = lax.axis_index("row")
    sent = []

    def start(copy):
        copy.start()
        sent.append(copy)
        return copy

    class Tower:
        pass

    ts = []
    for n, (place, full, early, late, pair, y_out, avg) in enumerate(
        (
            (one, t_one, early_one, late_one, pair_one, y_out_one, avg_one),
            (two, core_sum, early_two, late_two, pair_two, y_out_two, avg_two),
        )
    ):
        t = Tower()
        t.n, t.full, t.early, t.late, t.pair, t.y_out, t.avg = n, full, early, late, pair, y_out, avg
        t.__dict__.update(place)
        t.half = t.size // 2
        ts.append(t)

    def at(t, step, j, first, count):
        if t.n == 0:
            return t.full.at[pl.ds(t.rows((t.place + step) % 4, j) + first, count)]
        return t.full.at[(step * 2 + j), pl.ds(first, count)]

    def twin_rows(step, j, core):
        rows = ((two["place"] + step) % 4 * 4 + ((row // 2 + j) % 2) * 2 + core) * 128
        return t_two.at[pl.ds(pl.multiple_of(rows, 128), 128)]

    order = [(2, 1), (2, 0), (1, 1), (3, 1), (1, 0), (3, 0), (0, 1), (0, 0)]
    for step, j in order:
        slot = step * 2 + j
        start(
            remote(
                twin_rows(step, j, 1 - row % 2), core_in.at[slot], core_sem.at[0, slot], core_sem.at[1, slot], twin
            )
        )

    def send_early(t, j):
        for way, device in ((0, t.plus), (1, t.minus)):
            start(
                remote(
                    at(t, 2, j, way * t.half, t.half), t.early.at[j, way],
                    early_sem.at[0, t.n, j, way], early_sem.at[1, t.n, j, way], device,
                )
            )

    def send_plain(t, j):
        for way, device in ((0, t.plus), (1, t.minus)):
            other = 1 - way
            start(
                remote(
                    at(t, 1 if way == 0 else 3, j, other * t.half, t.half), t.late.at[j, way, other],
                    late_sem.at[0, t.n, j, way, other], late_sem.at[1, t.n, j, way, other], device,
                )
            )

    def send_joined(t, j):
        for way, device in ((0, t.plus), (1, t.minus)):
            buf = t.early.at[j, way]
            remote(
                buf, buf, early_sem.at[0, t.n, j, way], early_sem.at[1, t.n, j, way], device
            ).wait_recv()
            mine = at(t, 1 if way == 0 else 3, j, way * t.half, t.half)
            buf[...] = (mine[...].astype(F32) + buf[...].astype(F32)).astype(BF)
            start(
                remote(
                    buf, t.late.at[j, way, way],
                    late_sem.at[0, t.n, j, way, way], late_sem.at[1, t.n, j, way, way], device,
                )
            )

    def total(t, j):
        for way in range(2):
            for which in range(2):
                buf = t.late.at[j, way, which]
                remote(
                    buf, buf, late_sem.at[0, t.n, j, way, which], late_sem.at[1, t.n, j, way, which], twin
                ).wait_recv()
        full = []
        for which in range(2):
            full.append(
                at(t, 0, j, which * t.half, t.half)[...].astype(F32)
                + t.late[j, 0, which].astype(F32)
                + t.late[j, 1, which].astype(F32)
            )
        return full

    t1, t2 = ts
    for j in (1, 0):
        send_early(t1, j)
    for j in (1, 0):
        send_plain(t1, j)
    for step, j in order:
        slot = step * 2 + j
        remote(
            core_in.at[slot], core_in.at[slot], core_sem.at[0, slot], core_sem.at[1, slot], twin
        ).wait_recv()
        core_sum[slot] = (twin_rows(step, j, row % 2)[...].astype(F32) + core_in[slot].astype(F32)).astype(BF)
        if (step, j) in ((2, 1), (2, 0)):
            send_early(t2, j)
    for j in (1, 0):
        send_plain(t2, j)
    for j in (1, 0):
        for t in ts:
            send_joined(t, j)
    for t in (t2, t1):
        full = total(t, 1)
        for which in range(2):
            t.y_out[which * t.half : (which + 1) * t.half] = full[which].astype(BF)
        start(remote(t.y_out, t.pair, y_sem.at[0, t.n], y_sem.at[1, t.n], t.partner))
    for t in (t2, t1):
        full = total(t, 0)
        remote(t.pair, t.pair, y_sem.at[0, t.n], y_sem.at[1, t.n], t.partner).wait_recv()
        for which in range(2):
            rows = slice(which * t.half, (which + 1) * t.half)
            t.avg[rows] = full[which] + t.pair[rows].astype(F32)
    for copy in sent:
        copy.wait_send()


def reduce(t_one, t_two):
    sem = pltpu.SemaphoreType.DMA
    v = lambda *shape: pltpu.VMEM(shape, BF)
    return pl.pallas_call(
        reduce_kernel,
        out_shape=(jax.ShapeDtypeStruct((256, D), F32), jax.ShapeDtypeStruct((128, D), F32)),
        in_specs=[VMEM, VMEM],
        out_specs=(VMEM, VMEM),
        scratch_shapes=[
            v(2, 2, 128, D),
            v(2, 2, 64, D),
            v(2, 2, 2, 128, D),
            v(2, 2, 2, 64, D),
            v(256, D),
            v(128, D),
            v(8, 128, D),
            v(8, 128, D),
            v(256, D),
            v(128, D),
            sem((2, 2, 2, 2)),
            sem((2, 2, 2, 2, 2)),
            sem((2, 2)),
            sem((2, 8)),
        ],
        compiler_params=pltpu.CompilerParams(has_side_effects=True, vmem_limit_bytes=60 * 2**20),
        name="reduce",
    )(t_one, t_two)


def shards(documents, targets, routes, doc_counts, module_one, module_two, moment_one, moment_two):
    row_id = lax.axis_index("row")
    col_id = lax.axis_index("col")
    slots = pack(routes, documents, targets)
    w_one, w_two, got = gather(
        module_one[0].astype(BF), module_two[0].astype(BF), slots.reshape(PATHS, 8, D)
    )
    counts = doc_counts.astype(F32)
    row_counts = lax.dynamic_index_in_dim(counts, row_id, 0, keepdims=False)
    col_counts = lax.dynamic_index_in_dim(counts, col_id, 1, keepdims=False)
    own_count = lax.dynamic_index_in_dim(row_counts, col_id, 0, keepdims=False)
    share = jnp.stack([own_count / jnp.sum(row_counts), own_count / jnp.sum(col_counts)])
    t_one, t_two = compute(share, got.reshape(PATHS * 8, D), w_one, w_two)
    avg_one, avg_two = reduce(t_one, t_two)
    next_moment_one = outer_moment * moment_one + avg_one[None]
    next_moment_two = outer_moment * moment_two + avg_two[None]
    new_one = module_one - outer_rate * (outer_moment * next_moment_one + avg_one[None])
    new_two = module_two - outer_rate * (outer_moment * next_moment_two + avg_two[None])
    return (new_one, new_two, next_moment_one, next_moment_two)


def solution(mesh):
    return jax.shard_map(
        shards,
        mesh=mesh,
        in_specs=(
            P(None, ("row", "col"), None),
            P(None, ("row", "col"), None),
            P(None, ("row", "col"), None),
            P(),
            P("row", "col", None),
            P("col", "row", None),
            P("row", "col", None),
            P("col", "row", None),
        ),
        out_specs=(
            P("row", "col", None),
            P("col", "row", None),
            P("row", "col", None),
            P("col", "row", None),
        ),
        check_vma=False,
    )
```

```python
import functools

import jax
import jax.numpy as jnp
from jax import lax
from jax.experimental import pallas as pl
from jax.experimental.pallas import tpu as pltpu
from jax.sharding import PartitionSpec as P

D = 2048
ROWS = 128
PATHS = 128
SLOTS = 256
N_ROW = 16
N_COL = 8
SCALE = D ** (-0.5)
GUARD = 0.5 / (D * ROWS) ** 0.5 / SCALE

outer_rate = 0.7
outer_moment = 0.9

BF = jnp.bfloat16
F32 = jnp.float32
MESH = pl.DeviceIdType.MESH
ANY = pl.BlockSpec(memory_space=pl.ANY)
VMEM = pl.BlockSpec(memory_space=pltpu.VMEM)


def iota(shape, dim):
    return lax.broadcasted_iota(jnp.int32, shape, dim)


def pack_kernel(dest_col, dest_row, docs, targs, out):
    block = pl.program_id(0) % 4
    row = dest_row[0]
    same = jnp.where(dest_col[0] == row, 1, 0)
    earlier = jnp.where(iota((ROWS, ROWS), 0) < iota((ROWS, ROWS), 1), same, 0)
    rank = jnp.sum(earlier, axis=0, keepdims=True)
    total = jnp.zeros((256, D // 2), F32)
    for kind, source in enumerate((docs, targs)):
        for half in range(2):
            slot = row * 8 + (kind * 4 + half) + rank * 2 - block * 256
            pick = jnp.where(iota((256, ROWS), 0) == slot, 1.0, 0.0).astype(BF)
            total += jnp.dot(pick, source[0, :, half * 1024 : (half + 1) * 1024], preferred_element_type=F32)
    out[...] = total.astype(BF)


def pack(routes, docs, targs):
    return pl.pallas_call(
        pack_kernel,
        grid=(8,),
        out_shape=jax.ShapeDtypeStruct((2 * PATHS * 8, D // 2), BF),
        in_specs=[
            pl.BlockSpec((1, ROWS, 1), lambda i: (i // 4, 0, 0)),
            pl.BlockSpec((1, 1, ROWS), lambda i: (i // 4, 0, 0)),
            pl.BlockSpec((1, ROWS, D), lambda i: (i // 4, 0, 0)),
            pl.BlockSpec((1, ROWS, D), lambda i: (i // 4, 0, 0)),
        ],
        out_specs=pl.BlockSpec((256, D // 2), lambda i: (i, 0)),
        name="pack",
    )(routes, routes.reshape(2, 1, ROWS), docs, targs)


P_ROWS = 160
Q_ROWS = 256 - P_ROWS


class Stream:
    def __init__(self, **fields):
        self.__dict__.update(fields)

    def at(self, full, step, first, count):
        return full.at[pl.ds(pl.multiple_of(self.rows((self.place + step) % 4), 16) + first, count)]


def remote(src, dst, sems, device):
    return pltpu.make_async_remote_copy(
        src_ref=src, dst_ref=dst, send_sem=sems.at[0], recv_sem=sems.at[1], device_id=device, device_id_type=MESH
    )


def round_kernel(
    counts, own_one, own_two, slots, got, avg_one, avg_two,
    one, two, g_one, g_two, stage, x, y, hid, err, inn, slope, x_t, h_t,
    early_p, late_p, pair_p, y_q, early_q, late_q, core_in, early_t, late_t, pair_t,
    ring_sem, fwd_sem, y_sem, q_sem, core_sem, a2a_sem, local_sem,
    early_sem, late_sem, pair_sem, yq_sem, core_two_sem,
):
    row, col = lax.axis_index("row"), lax.axis_index("col")
    xx, low, core = row // 4, (row // 2) % 2, row % 2
    z, high = col // 2, col % 2
    me = row * N_COL + col

    def device(x=xx, low=low, core=core, z=z, high=high):
        return (x * 4 + low * 2 + core, z * 2 + high)

    twin = device(core=1 - core)
    ring_one = dict(place=z, plus=device(z=(z + 1) % 4), minus=device(z=(z + 3) % 4), partner=device(high=1 - high))
    ring_two = dict(place=xx, plus=device(x=(xx + 1) % 4), minus=device(x=(xx + 3) % 4), partner=device(low=1 - low))

    def rows_one(first, j):
        return lambda place: (place * 2 + (high + j) % 2) * 256 + first

    def rows_two(j, core=core):
        return lambda place: (place * 4 + ((low + j) % 2) * 2 + core) * 128

    p0 = Stream(n=0, half=P_ROWS // 2, rows=rows_one(0, 0), **ring_one)
    p1 = Stream(n=1, half=P_ROWS // 2, rows=rows_one(0, 1), **ring_one)
    q0 = Stream(n=2, half=Q_ROWS // 2, rows=rows_one(P_ROWS, 0), **ring_one)
    q1 = Stream(half=Q_ROWS // 2, rows=rows_one(P_ROWS, 1), **ring_one)
    t0 = Stream(n=3, half=64, rows=rows_two(0), **ring_two)
    t1 = Stream(n=4, half=64, rows=rows_two(1), **ring_two)
    u0 = Stream(half=64, rows=rows_two(0, 1 - core), **ring_two)
    u1 = Stream(half=64, rows=rows_two(1, 1 - core), **ring_two)
    sent = []

    def start(copy):
        copy.start()
        sent.append(copy)

    def whole(s, full, step):
        return s.at(full, step, 0, 2 * s.half)

    def spread(s, full, own=None):
        for way, to in ((0, s.plus), (1, s.minus)):
            for which in (0, 1) if way == 0 else (1, 0):
                dst = s.at(full, 0, which * s.half, s.half)
                src = dst if own is None else own.at[pl.ds(which * s.half, s.half)]
                start(remote(src, dst, ring_sem.at[s.n, way, which], to))

    def arrived(s, full, way, which):
        ref = s.at(full, 3 if way == 0 else 1, which * s.half, s.half)
        remote(ref, ref, ring_sem.at[s.n, way, which], twin).wait_recv()

    def forward(s, full):
        for way, to in ((0, s.plus), (1, s.minus)):
            arrived(s, full, way, way)
            ref = s.at(full, 3 if way == 0 else 1, way * s.half, s.half)
            start(remote(ref, ref, fwd_sem.at[s.n, way], to))

    def rest(s, full):
        arrived(s, full, 0, 1)
        arrived(s, full, 1, 0)

    def forwarded(s, full):
        for way in range(2):
            ref = s.at(full, 2, way * s.half, s.half)
            remote(ref, ref, fwd_sem.at[s.n, way], twin).wait_recv()

    def q_across(step, src=None):
        dst = whole(q0, one, step)
        start(remote(dst if src is None else src, dst, q_sem.at[step], q0.partner))

    def to_twin(s, j, step, src=None):
        dst = whole(s, two, step)
        start(remote(dst if src is None else src, dst, core_sem.at[step, j], twin))

    own_p, own_q = own_one.at[pl.ds(0, P_ROWS)], own_one.at[pl.ds(P_ROWS, Q_ROWS)]
    start(remote(own_p, whole(p0, one, 0), y_sem.at[0], p0.partner))
    start(remote(own_two, whole(t0, two, 0), y_sem.at[1], t0.partner))
    spread(p0, one, own_p)
    spread(t0, two, own_two)
    spread(q0, one, own_q)
    q_across(0, own_q)
    to_twin(t0, 0, 0, own_two)
    locals_ = [
        pltpu.make_async_copy(own_p, whole(p0, one, 0), local_sem.at[0]),
        pltpu.make_async_copy(own_q, whole(q0, one, 0), local_sem.at[1]),
        pltpu.make_async_copy(own_two, whole(t0, two, 0), local_sem.at[2]),
        pltpu.make_async_copy(slots.at[0, me], got.at[0, me], local_sem.at[3]),
        pltpu.make_async_copy(slots.at[1, me], got.at[1, me], local_sem.at[4]),
    ]
    for copy in locals_:
        copy.start()

    def send_slots(m):
        def send(step, carry):
            t = step * 53 % PATHS
            to = device(
                x=(xx + t % 4) % 4,
                low=(low + t // 4 % 2) % 2,
                high=(high + t // 8 % 2) % 2,
                z=(z + t // 16 % 4) % 4,
                core=(core + t // 64) % 2,
            )
            remote(slots.at[m, to[0] * N_COL + to[1]], got.at[m, me], a2a_sem.at[m], to).start()
            return carry

        lax.fori_loop(1, PATHS, send, 0)

    def all_slots(m):
        return remote(slots.at[m, pl.ds(0, PATHS - 1)], got.at[m, pl.ds(0, PATHS - 1)], a2a_sem.at[m], twin)

    send_slots(0)
    remote(own_p, whole(p1, one, 0), y_sem.at[0], twin).wait_recv()
    spread(p1, one)
    remote(own_two, whole(t1, two, 0), y_sem.at[1], twin).wait_recv()
    spread(t1, two)
    to_twin(t1, 1, 0)
    forward(p0, one)
    forward(t0, two)
    forward(q0, one)
    forward(p1, one)
    forward(t1, two)
    rest(q0, one)
    q_across(1)
    q_across(3)
    for j, s in ((0, t0), (1, t1)):
        rest(s, two)
        to_twin(s, j, 1)
        to_twin(s, j, 3)
    forwarded(q0, one)
    q_across(2)
    for j, s in ((0, t0), (1, t1)):
        forwarded(s, two)
        to_twin(s, j, 2)
    send_slots(1)
    for step in range(4):
        ref = whole(q1, one, step)
        remote(ref, ref, q_sem.at[step], twin).wait_recv()
        for j, s in ((0, u0), (1, u1)):
            ref = whole(s, two, step)
            remote(ref, ref, core_sem.at[step, j], twin).wait_recv()
    for s in (p0, p1):
        rest(s, one)
        forwarded(s, one)
    for copy in locals_:
        copy.wait()
    all_slots(0).wait_recv()

    def unpack(m):
        o, i = iota((256, 256), 0), iota((256, 256), 1)
        source = o % 64 // 2 * 8 + o // 128 * 4 + o % 2 * 2 + o // 64 % 2
        pick = jnp.where(i == source, 1.0, 0.0).astype(BF)
        loads = [
            pltpu.make_async_copy(got.at[m, pl.ds(b * 32, 32)], stage.at[b % 2], local_sem.at[5 + b % 2]) for b in range(4)
        ]
        loads[0].start()
        loads[1].start()
        for b in range(4):
            loads[b].wait()
            part = stage[b % 2].reshape(256, D // 2)
            rows = jnp.dot(pick, part, preferred_element_type=F32).astype(BF)
            for half in range(2):
                cols = slice(half * 1024, (half + 1) * 1024)
                x[b * 64 : (b + 1) * 64, cols] = rows[half * 64 : half * 64 + 64]
                y[b * 64 : (b + 1) * 64, cols] = rows[128 + half * 64 : 192 + half * 64]
            if b < 2:
                loads[b + 2].start()

    def spans(n, tile):
        return pl.ds(pl.multiple_of(n * tile, tile), tile)

    def passes():
        wide = 1024

        def pre_tile(n, carry):
            cols = spans(n, wide)
            pre = jnp.dot(x[...], one[:, cols], preferred_element_type=F32) * SCALE
            sig = 1.0 / (1.0 + jnp.exp(-pre))
            hid[:, cols] = (pre * sig).astype(BF)
            slope[:, cols] = sig * (1.0 + pre * (1.0 - sig))
            return carry

        lax.fori_loop(0, D // wide, pre_tile, 0)

        def err_tile(n, carry):
            cols = spans(n, wide)
            out = jnp.dot(hid[...], two[:, cols], preferred_element_type=F32) * SCALE
            out = x[:, cols].astype(F32) + out
            err[:, cols] = ((out - y[:, cols].astype(F32)) / ROWS).astype(BF)
            return carry

        lax.fori_loop(0, D // wide, err_tile, 0)

        def inn_tile(n, carry):
            cols = spans(n, wide)
            back = lax.dot_general(err[...], two[cols, :], (((1,), (1,)), ((), ())), preferred_element_type=F32)
            inn[:, cols] = (back * SCALE * slope[:, cols]).astype(BF)
            return carry

        lax.fori_loop(0, D // wide, inn_tile, 0)

        def turn(n, carry):
            cols = spans(n, 256)
            x_t[cols, :] = x[:, cols].T
            h_t[cols, :] = hid[:, cols].T
            return carry

        lax.fori_loop(0, D // 256, turn, 0)

    def first_update(left, right, w, g):
        def step(n, carry):
            rows, cols = spans(n // 4, 1024), spans(n % 4, 512)
            grad = jnp.dot(left[rows, :], right[:, cols], preferred_element_type=F32)
            update = grad / (jnp.abs(grad) + GUARD)
            g[rows, cols] = grad.astype(BF)
            w[rows, cols] = (0.99 * w[rows, cols].astype(F32) - 0.1 * update).astype(BF)
            return carry

        lax.fori_loop(0, 8, step, 0)

    tally = counts[...].astype(F32)
    in_row = jnp.where(iota((N_ROW, N_COL), 0) == row, tally, 0.0)
    in_col = jnp.where(iota((N_ROW, N_COL), 1) == col, tally, 0.0)
    mine = jnp.where(iota((N_ROW, N_COL), 1) == col, in_row, 0.0)

    def grand(v):
        return jnp.sum(jnp.sum(v, axis=0, keepdims=True), axis=1, keepdims=True)

    share_one, share_two = grand(mine) / grand(in_row), grand(mine) / grand(in_col)
    root = (0.05 / 0.0975) ** 0.5

    def last_update(left, right, w, g, weight, first_row):
        part_w, part_a = weight * (1.0 / 0.99 - 0.99), weight * (0.1 / 0.99)
        part_b = weight * (0.1 * (0.1 / 0.19) / root)

        def step(n, carry):
            rows, cols = pl.ds(pl.multiple_of(first_row, 512), 512), spans(n, 512)
            grad = jnp.dot(left[rows, :], right[:, cols], preferred_element_type=F32)
            before = g[rows, cols].astype(F32)
            update_a = before / (jnp.abs(before) + GUARD)
            second = 0.95 * (before * before) + grad * grad
            update_b = (0.9 * before + grad) / (jnp.sqrt(second) + GUARD / root)
            g[rows, cols] = (
                part_w * w[rows, cols].astype(F32) + part_a * update_a + part_b * update_b
            ).astype(BF)
            return carry

        lax.fori_loop(0, 4, step, 0)

    unpack(0)
    passes()
    for copy in sent:
        copy.wait_send()
    sent.clear()
    first_update(h_t, err, two, g_two)
    first_update(x_t, inn, one, g_one)
    all_slots(1).wait_recv()
    unpack(1)
    passes()

    for s, full, early, late in (
        (p0, g_one, early_p.at[0], late_p.at[0]),
        (p1, g_one, early_p.at[1], late_p.at[1]),
        (q0, g_one, early_q, late_q),
        (t0, g_two, early_t.at[0], late_t.at[0]),
        (t1, g_two, early_t.at[1], late_t.at[1]),
    ):
        s.full, s.early, s.late = full, early, late

    def send_early(s):
        for way, to in ((0, s.plus), (1, s.minus)):
            src = s.at(s.full, 2, way * s.half, s.half)
            start(remote(src, s.early.at[way], early_sem.at[s.n, way], to))

    def send_plain(s, way):
        other = 1 - way
        src = s.at(s.full, 1 if way == 0 else 3, other * s.half, s.half)
        to = s.plus if way == 0 else s.minus
        start(remote(src, s.late.at[way, other], late_sem.at[s.n, way, other], to))

    def send_joined(s):
        for way, to in ((0, s.plus), (1, s.minus)):
            buf = s.early.at[way]
            remote(buf, buf, early_sem.at[s.n, way], twin).wait_recv()
            mine = s.at(s.full, 1 if way == 0 else 3, way * s.half, s.half)
            buf[...] = (mine[...].astype(F32) + buf[...].astype(F32)).astype(BF)
            start(remote(buf, s.late.at[way, way], late_sem.at[s.n, way, way], to))

    def total(s, which):
        for way in range(2):
            buf = s.late.at[way, which]
            remote(buf, buf, late_sem.at[s.n, way, which], twin).wait_recv()
        return (
            s.at(s.full, 0, which * s.half, s.half)[...].astype(F32)
            + s.late.at[0, which][...].astype(F32)
            + s.late.at[1, which][...].astype(F32)
        )

    def join_q(step):
        buf = y_q.at[step]
        remote(buf, buf, yq_sem.at[step], twin).wait_recv()
        mine = whole(q0, g_one, step)
        mine[...] = (mine[...].astype(F32) + buf[...].astype(F32)).astype(BF)

    def join_core(s, j, step):
        buf = core_in.at[step, j]
        remote(buf, buf, core_two_sem.at[step, j], twin).wait_recv()
        mine = whole(s, g_two, step)
        mine[...] = (mine[...].astype(F32) + buf[...].astype(F32)).astype(BF)

    def unit_one(step):
        last_update(x_t, inn, one, g_one, share_one, (z + step) % 4 * 512)
        start(remote(whole(q1, g_one, step), y_q.at[step], yq_sem.at[step], q1.partner))
        for s in (p1, p0):
            if step == 2:
                send_early(s)
            elif step:
                send_plain(s, step // 2)

    def unit_two(step):
        last_update(h_t, err, two, g_two, share_two, (xx + step) % 4 * 512)
        for j, s in ((1, u1), (0, u0)):
            start(remote(whole(s, g_two, step), core_in.at[step, j], core_two_sem.at[step, j], twin))

    for step in (2, 1, 3, 0):
        unit_one(step)
    unit_two(2)
    join_q(2)
    send_early(q0)
    join_q(1)
    send_plain(q0, 0)
    join_q(3)
    send_plain(q0, 1)
    for s in (p1, p0):
        send_joined(s)
    for j, s in ((1, t1), (0, t0)):
        join_core(s, j, 2)
        send_early(s)
    unit_two(1)
    for j, s in ((1, t1), (0, t0)):
        join_core(s, j, 1)
        send_plain(s, 0)
    unit_two(3)
    for j, s in ((1, t1), (0, t0)):
        join_core(s, j, 3)
        send_plain(s, 1)
    send_joined(q0)
    unit_two(0)
    join_q(0)
    for j, s in ((1, t1), (0, t0)):
        join_core(s, j, 0)
        send_joined(s)
    out_t, out_p = y.at[pl.ds(0, 128)], x.at[pl.ds(0, P_ROWS)]
    for s, out, pair, n in ((t1, out_t, pair_t, 1), (p1, out_p, pair_p, 0)):
        for which in range(2):
            out[which * s.half : (which + 1) * s.half] = total(s, which).astype(BF)
        start(remote(out, pair, pair_sem.at[n], s.partner))
    for which in range(2):
        first = P_ROWS + which * q0.half
        slope[first : first + q0.half] = total(q0, which)
    done = pltpu.make_async_copy(slope.at[pl.ds(0, 128)], avg_two, local_sem.at[5])
    for s, out, pair, n in ((t0, out_t, pair_t, 1), (p0, out_p, pair_p, 0)):
        full = [total(s, which) for which in range(2)]
        remote(out, pair, pair_sem.at[n], twin).wait_recv()
        if n == 0:
            done.wait()
        for which in range(2):
            rows = slice(which * s.half, (which + 1) * s.half)
            slope[rows] = full[which] + pair[rows].astype(F32)
        if n == 1:
            done.start()
    done = pltpu.make_async_copy(slope, avg_one, local_sem.at[5])
    done.start()
    for copy in sent:
        copy.wait_send()
    for m in range(2):
        all_slots(m).wait_send()
    done.wait()


def one_round(counts, own_one, own_two, slots):
    sem = pltpu.SemaphoreType.DMA
    v = lambda *shape: pltpu.VMEM(shape, BF)
    act = v(SLOTS, D)
    p, q = P_ROWS // 2, Q_ROWS // 2
    return pl.pallas_call(
        round_kernel,
        out_shape=(
            jax.ShapeDtypeStruct((2, PATHS, 8, D // 2), BF),
            jax.ShapeDtypeStruct((256, D), F32),
            jax.ShapeDtypeStruct((128, D), F32),
        ),
        in_specs=[VMEM, ANY, ANY, ANY],
        out_specs=(ANY, ANY, ANY),
        scratch_shapes=[v(D, D)] * 4
        + [v(2, 32, 8, D // 2)]
        + [act] * 5
        + [pltpu.VMEM((SLOTS, D), F32)]
        + [v(D, SLOTS)] * 2
        + [v(2, 2, p, D), v(2, 2, 2, p, D), v(2 * p, D)]
        + [v(4, 2 * q, D), v(2, q, D), v(2, 2, q, D)]
        + [v(4, 2, 128, D), v(2, 2, 64, D), v(2, 2, 2, 64, D), v(128, D)]
        + [sem((5, 2, 2, 2)), sem((5, 2, 2)), sem((2, 2)), sem((4, 2)), sem((4, 2, 2)), sem((2, 2)), sem((7,))]
        + [sem((5, 2, 2)), sem((5, 2, 2, 2)), sem((2, 2)), sem((4, 2)), sem((4, 2, 2))],
        compiler_params=pltpu.CompilerParams(has_side_effects=True, vmem_limit_bytes=67043328),
        name="round",
    )(counts, own_one, own_two, slots)


def shards(documents, targets, routes, doc_counts, module_one, module_two, moment_one, moment_two):
    slots = pack(routes, documents, targets)
    got, avg_one, avg_two = one_round(
        doc_counts, module_one[0].astype(BF), module_two[0].astype(BF), slots.reshape(2, PATHS, 8, D // 2)
    )
    next_moment_one = outer_moment * moment_one + avg_one[None]
    next_moment_two = outer_moment * moment_two + avg_two[None]
    new_one = module_one - outer_rate * (outer_moment * next_moment_one + avg_one[None])
    new_two = module_two - outer_rate * (outer_moment * next_moment_two + avg_two[None])
    return (new_one, new_two, next_moment_one, next_moment_two)


def solution(mesh):
    return jax.shard_map(
        shards,
        mesh=mesh,
        in_specs=(
            P(None, ("row", "col"), None),
            P(None, ("row", "col"), None),
            P(None, ("row", "col"), None),
            P(),
            P("row", "col", None),
            P("col", "row", None),
            P("row", "col", None),
            P("col", "row", None),
        ),
        out_specs=(
            P("row", "col", None),
            P("col", "row", None),
            P("row", "col", None),
            P("col", "row", None),
        ),
        check_vma=False,
    )
```

```python
import functools

import jax
import jax.numpy as jnp
from jax import lax
from jax.experimental import pallas as pl
from jax.experimental.pallas import tpu as pltpu
from jax.sharding import PartitionSpec as P

D = 2048
ROWS = 128
PATHS = 128
SLOTS = 256
N_ROW = 16
N_COL = 8
SCALE = D ** (-0.5)
GUARD = 0.5 / (D * ROWS) ** 0.5 / SCALE

outer_rate = 0.7
outer_moment = 0.9

BF = jnp.bfloat16
F32 = jnp.float32
MESH = pl.DeviceIdType.MESH
ANY = pl.BlockSpec(memory_space=pl.ANY)
VMEM = pl.BlockSpec(memory_space=pltpu.VMEM)


def iota(shape, dim):
    return lax.broadcasted_iota(jnp.int32, shape, dim)


P_ROWS = 160
Q_ROWS = 256 - P_ROWS


class Stream:
    def __init__(self, **fields):
        self.__dict__.update(fields)

    def at(self, full, step, first, count):
        return full.at[pl.ds(pl.multiple_of(self.rows((self.place + step) % 4), 16) + first, count)]


def remote(src, dst, sems, device):
    return pltpu.make_async_remote_copy(
        src_ref=src, dst_ref=dst, send_sem=sems.at[0], recv_sem=sems.at[1], device_id=device, device_id_type=MESH
    )


def round_kernel(
    routes, counts_in, docs, targs, module_one, module_two, got, avg_one, avg_two,
    counts,
    one, two, g_one, g_two, stage, x, y, hid, err, inn, slope, x_t, h_t,
    early_p, late_p, pair_p, y_q, early_q, late_q, core_in, early_t, late_t, pair_t,
    ring_sem, fwd_sem, y_sem, q_sem, core_sem, a2a_sem, local_sem,
    early_sem, late_sem, pair_sem, yq_sem, core_two_sem,
):
    row, col = lax.axis_index("row"), lax.axis_index("col")
    xx, low, core = row // 4, (row // 2) % 2, row % 2
    z, high = col // 2, col % 2
    me = row * N_COL + col

    def device(x=xx, low=low, core=core, z=z, high=high):
        return (x * 4 + low * 2 + core, z * 2 + high)

    twin = device(core=1 - core)
    ring_one = dict(place=z, plus=device(z=(z + 1) % 4), minus=device(z=(z + 3) % 4), partner=device(high=1 - high))
    ring_two = dict(place=xx, plus=device(x=(xx + 1) % 4), minus=device(x=(xx + 3) % 4), partner=device(low=1 - low))

    def rows_one(first, j):
        return lambda place: (place * 2 + (high + j) % 2) * 256 + first

    def rows_two(j, core=core):
        return lambda place: (place * 4 + ((low + j) % 2) * 2 + core) * 128

    p0 = Stream(n=0, half=P_ROWS // 2, rows=rows_one(0, 0), **ring_one)
    p1 = Stream(n=1, half=P_ROWS // 2, rows=rows_one(0, 1), **ring_one)
    q0 = Stream(n=2, half=Q_ROWS // 2, rows=rows_one(P_ROWS, 0), **ring_one)
    q1 = Stream(half=Q_ROWS // 2, rows=rows_one(P_ROWS, 1), **ring_one)
    t0 = Stream(n=3, half=64, rows=rows_two(0), **ring_two)
    t1 = Stream(n=4, half=64, rows=rows_two(1), **ring_two)
    u0 = Stream(half=64, rows=rows_two(0, 1 - core), **ring_two)
    u1 = Stream(half=64, rows=rows_two(1, 1 - core), **ring_two)
    sent = []

    def start(copy):
        copy.start()
        sent.append(copy)

    def whole(s, full, step):
        return s.at(full, step, 0, 2 * s.half)

    def spread(s, full):
        for way, to in ((0, s.plus), (1, s.minus)):
            for which in (0, 1) if way == 0 else (1, 0):
                ref = s.at(full, 0, which * s.half, s.half)
                start(remote(ref, ref, ring_sem.at[s.n, way, which], to))

    def arrived(s, full, way, which):
        ref = s.at(full, 3 if way == 0 else 1, which * s.half, s.half)
        remote(ref, ref, ring_sem.at[s.n, way, which], twin).wait_recv()

    def forward(s, full):
        for way, to in ((0, s.plus), (1, s.minus)):
            arrived(s, full, way, way)
            ref = s.at(full, 3 if way == 0 else 1, way * s.half, s.half)
            start(remote(ref, ref, fwd_sem.at[s.n, way], to))

    def rest(s, full):
        arrived(s, full, 0, 1)
        arrived(s, full, 1, 0)

    def forwarded(s, full):
        for way in range(2):
            ref = s.at(full, 2, way * s.half, s.half)
            remote(ref, ref, fwd_sem.at[s.n, way], twin).wait_recv()

    def q_across(step):
        ref = whole(q0, one, step)
        start(remote(ref, ref, q_sem.at[step], q0.partner))

    def to_twin(s, j, step):
        ref = whole(s, two, step)
        start(remote(ref, ref, core_sem.at[step, j], twin))

    def unpack(m):
        o, i = iota((256, 256), 0), iota((256, 256), 1)
        source = o % 64 // 2 * 8 + o // 128 * 4 + o % 2 * 2 + o // 64 % 2
        pick = jnp.where(i == source, 1.0, 0.0).astype(BF)
        loads = [
            pltpu.make_async_copy(got.at[m, pl.ds(b * 32, 32)], stage.at[b % 2], local_sem.at[5 + b % 2]) for b in range(4)
        ]
        loads[0].start()
        loads[1].start()
        for b in range(4):
            loads[b].wait()
            part = stage[b % 2].reshape(256, D // 2)
            rows = jnp.dot(pick, part, preferred_element_type=F32).astype(BF)
            for half in range(2):
                cols = slice(half * 1024, (half + 1) * 1024)
                x[b * 64 : (b + 1) * 64, cols] = rows[half * 64 : half * 64 + 64]
                y[b * 64 : (b + 1) * 64, cols] = rows[128 + half * 64 : 192 + half * 64]
            if b < 2:
                loads[b + 2].start()

    upper = pltpu.make_async_copy(module_one.at[0, pl.ds(0, 128)], slope.at[pl.ds(0, 128)], local_sem.at[0])
    lower = pltpu.make_async_copy(module_one.at[0, pl.ds(128, 128)], slope.at[pl.ds(0, 128)], local_sem.at[1])
    other = pltpu.make_async_copy(module_two.at[0], slope.at[pl.ds(128, 128)], local_sem.at[2])
    upper.start()
    other.start()
    loads = [
        pltpu.make_async_copy(source.at[m], to.at[pl.ds(m * ROWS, ROWS)], local_sem.at[3 + m * 2 + n])
        for m in range(2)
        for n, (source, to) in enumerate(((docs, x), (targs, y)))
    ]
    loads.append(pltpu.make_async_copy(counts_in, counts, local_sem.at[7]))
    for copy in loads:
        copy.start()
    upper.wait()
    p0.at(one, 0, 0, 128)[...] = slope[0:128].astype(BF)
    lower.start()
    other.wait()
    whole(t0, two, 0)[...] = slope[128:256].astype(BF)
    start(remote(whole(t0, two, 0), whole(t0, two, 0), y_sem.at[1], t0.partner))
    lower.wait()
    p0.at(one, 0, 128, 128)[...] = slope[0:128].astype(BF)
    start(remote(whole(p0, one, 0), whole(p0, one, 0), y_sem.at[0], p0.partner))
    spread(p0, one)
    spread(t0, two)
    spread(q0, one)
    q_across(0)
    to_twin(t0, 0, 0)
    for copy in loads:
        copy.wait()

    def pack(m):
        to = routes[m]
        same_place = iota((ROWS, ROWS), 0) == iota((ROWS, ROWS), 1)
        down = jnp.sum(jnp.where(same_place, to, 0), axis=1, keepdims=True)
        same = jnp.where(down == to, 1, 0)
        earlier = jnp.where(iota((ROWS, ROWS), 0) < iota((ROWS, ROWS), 1), same, 0)
        rank = jnp.sum(earlier, axis=0, keepdims=True)

        def block(b, carry):
            total = jnp.zeros((256, D // 2), F32)
            for kind, source in enumerate((x, y)):
                for half in range(2):
                    slot = to * 8 + (kind * 4 + half) + rank * 2 - b * 256
                    pick = jnp.where(iota((256, ROWS), 0) == slot, 1.0, 0.0).astype(BF)
                    part = source[m * ROWS : (m + 1) * ROWS, half * 1024 : (half + 1) * 1024]
                    total += jnp.dot(pick, part, preferred_element_type=F32)
            g_one[pl.ds(pl.multiple_of(b * 256, 256), 256), m * 1024 : (m + 1) * 1024] = total.astype(BF)
            return carry

        lax.fori_loop(0, 4, block, 0)

    def slot_rows(m, path):
        return g_one.at[pl.ds(pl.multiple_of(path * 8, 8), 8), pl.ds(m * 1024, 1024)]

    def send_slots(m):
        def send(step, carry):
            t = step * 53 % PATHS
            to = device(
                x=(xx + t % 4) % 4,
                low=(low + t // 4 % 2) % 2,
                high=(high + t // 8 % 2) % 2,
                z=(z + t // 16 % 4) % 4,
                core=(core + t // 64) % 2,
            )
            remote(slot_rows(m, to[0] * N_COL + to[1]), got.at[m, me], a2a_sem.at[m], to).start()
            return carry

        lax.fori_loop(1, PATHS, send, 0)

    def all_slots(m):
        ref = got.at[m, pl.ds(0, PATHS - 1)]
        return remote(ref, ref, a2a_sem.at[m], twin)

    own_slots = [pltpu.make_async_copy(slot_rows(m, me), got.at[m, me], local_sem.at[m]) for m in range(2)]
    for m in range(2):
        pack(m)
        own_slots[m].start()
        if m == 0:
            send_slots(0)
    remote(whole(p1, one, 0), whole(p1, one, 0), y_sem.at[0], twin).wait_recv()
    spread(p1, one)
    remote(whole(t1, two, 0), whole(t1, two, 0), y_sem.at[1], twin).wait_recv()
    spread(t1, two)
    to_twin(t1, 1, 0)
    forward(p0, one)
    forward(t0, two)
    forward(q0, one)
    forward(p1, one)
    forward(t1, two)
    rest(q0, one)
    q_across(1)
    q_across(3)
    for j, s in ((0, t0), (1, t1)):
        rest(s, two)
        to_twin(s, j, 1)
        to_twin(s, j, 3)
    forwarded(q0, one)
    q_across(2)
    for j, s in ((0, t0), (1, t1)):
        forwarded(s, two)
        to_twin(s, j, 2)
    for copy in own_slots:
        copy.wait()
    all_slots(0).wait_recv()
    unpack(0)
    for step in range(4):
        ref = whole(q1, one, step)
        remote(ref, ref, q_sem.at[step], twin).wait_recv()
        for j, s in ((0, u0), (1, u1)):
            ref = whole(s, two, step)
            remote(ref, ref, core_sem.at[step, j], twin).wait_recv()
    for s in (p0, p1):
        rest(s, one)
        forwarded(s, one)
    send_slots(1)

    def spans(n, tile):
        return pl.ds(pl.multiple_of(n * tile, tile), tile)

    def passes():
        wide = 1024

        def pre_tile(n, carry):
            cols = spans(n, wide)
            pre = jnp.dot(x[...], one[:, cols], preferred_element_type=F32) * SCALE
            sig = 1.0 / (1.0 + jnp.exp(-pre))
            hid[:, cols] = (pre * sig).astype(BF)
            slope[:, cols] = sig * (1.0 + pre * (1.0 - sig))
            return carry

        lax.fori_loop(0, D // wide, pre_tile, 0)

        def err_tile(n, carry):
            cols = spans(n, wide)
            out = jnp.dot(hid[...], two[:, cols], preferred_element_type=F32) * SCALE
            out = x[:, cols].astype(F32) + out
            err[:, cols] = ((out - y[:, cols].astype(F32)) / ROWS).astype(BF)
            return carry

        lax.fori_loop(0, D // wide, err_tile, 0)

        def inn_tile(n, carry):
            cols = spans(n, wide)
            back = lax.dot_general(err[...], two[cols, :], (((1,), (1,)), ((), ())), preferred_element_type=F32)
            inn[:, cols] = (back * SCALE * slope[:, cols]).astype(BF)
            return carry

        lax.fori_loop(0, D // wide, inn_tile, 0)

        def turn(n, carry):
            cols = spans(n, 256)
            x_t[cols, :] = x[:, cols].T
            h_t[cols, :] = hid[:, cols].T
            return carry

        lax.fori_loop(0, D // 256, turn, 0)

    def first_update(left, right, w, g):
        def step(n, carry):
            rows, cols = spans(n // 4, 1024), spans(n % 4, 512)
            grad = jnp.dot(left[rows, :], right[:, cols], preferred_element_type=F32)
            update = grad / (jnp.abs(grad) + GUARD)
            g[rows, cols] = grad.astype(BF)
            w[rows, cols] = (0.99 * w[rows, cols].astype(F32) - 0.1 * update).astype(BF)
            return carry

        lax.fori_loop(0, 8, step, 0)

    tally = counts[...].astype(F32)
    in_row = jnp.where(iota((N_ROW, N_COL), 0) == row, tally, 0.0)
    in_col = jnp.where(iota((N_ROW, N_COL), 1) == col, tally, 0.0)
    mine = jnp.where(iota((N_ROW, N_COL), 1) == col, in_row, 0.0)

    def grand(v):
        return jnp.sum(jnp.sum(v, axis=0, keepdims=True), axis=1, keepdims=True)

    share_one, share_two = grand(mine) / grand(in_row), grand(mine) / grand(in_col)
    root = (0.05 / 0.0975) ** 0.5

    def last_update(left, right, w, g, weight, first_row):
        part_w, part_a = weight * (1.0 / 0.99 - 0.99), weight * (0.1 / 0.99)
        part_b = weight * (0.1 * (0.1 / 0.19) / root)

        def step(n, carry):
            rows, cols = pl.ds(pl.multiple_of(first_row, 512), 512), spans(n, 512)
            grad = jnp.dot(left[rows, :], right[:, cols], preferred_element_type=F32)
            before = g[rows, cols].astype(F32)
            update_a = before / (jnp.abs(before) + GUARD)
            second = 0.95 * (before * before) + grad * grad
            update_b = (0.9 * before + grad) / (jnp.sqrt(second) + GUARD / root)
            g[rows, cols] = (
                part_w * w[rows, cols].astype(F32) + part_a * update_a + part_b * update_b
            ).astype(BF)
            return carry

        lax.fori_loop(0, 4, step, 0)

    passes()
    for copy in sent:
        copy.wait_send()
    sent.clear()
    first_update(h_t, err, two, g_two)
    for m in range(2):
        all_slots(m).wait_send()
    first_update(x_t, inn, one, g_one)
    all_slots(1).wait_recv()
    unpack(1)
    passes()

    for s, full, early, late in (
        (p0, g_one, early_p.at[0], late_p.at[0]),
        (p1, g_one, early_p.at[1], late_p.at[1]),
        (q0, g_one, early_q, late_q),
        (t0, g_two, early_t.at[0], late_t.at[0]),
        (t1, g_two, early_t.at[1], late_t.at[1]),
    ):
        s.full, s.early, s.late = full, early, late

    def send_early(s):
        for way, to in ((0, s.plus), (1, s.minus)):
            src = s.at(s.full, 2, way * s.half, s.half)
            start(remote(src, s.early.at[way], early_sem.at[s.n, way], to))

    def send_plain(s, way):
        other = 1 - way
        src = s.at(s.full, 1 if way == 0 else 3, other * s.half, s.half)
        to = s.plus if way == 0 else s.minus
        start(remote(src, s.late.at[way, other], late_sem.at[s.n, way, other], to))

    def send_joined(s):
        for way, to in ((0, s.plus), (1, s.minus)):
            buf = s.early.at[way]
            remote(buf, buf, early_sem.at[s.n, way], twin).wait_recv()
            mine = s.at(s.full, 1 if way == 0 else 3, way * s.half, s.half)
            buf[...] = (mine[...].astype(F32) + buf[...].astype(F32)).astype(BF)
            start(remote(buf, s.late.at[way, way], late_sem.at[s.n, way, way], to))

    def total(s, which):
        for way in range(2):
            buf = s.late.at[way, which]
            remote(buf, buf, late_sem.at[s.n, way, which], twin).wait_recv()
        return (
            s.at(s.full, 0, which * s.half, s.half)[...].astype(F32)
            + s.late.at[0, which][...].astype(F32)
            + s.late.at[1, which][...].astype(F32)
        )

    def join_q(step):
        buf = y_q.at[step]
        remote(buf, buf, yq_sem.at[step], twin).wait_recv()
        mine = whole(q0, g_one, step)
        mine[...] = (mine[...].astype(F32) + buf[...].astype(F32)).astype(BF)

    def join_core(s, j, step):
        buf = core_in.at[step, j]
        remote(buf, buf, core_two_sem.at[step, j], twin).wait_recv()
        mine = whole(s, g_two, step)
        mine[...] = (mine[...].astype(F32) + buf[...].astype(F32)).astype(BF)

    def unit_one(step):
        last_update(x_t, inn, one, g_one, share_one, (z + step) % 4 * 512)
        start(remote(whole(q1, g_one, step), y_q.at[step], yq_sem.at[step], q1.partner))

    def unit_two(step):
        last_update(h_t, err, two, g_two, share_two, (xx + step) % 4 * 512)
        for j, s in ((1, u1), (0, u0)):
            start(remote(whole(s, g_two, step), core_in.at[step, j], core_two_sem.at[step, j], twin))

    def to_pair(s, out, pair, n):
        for which in range(2):
            out[which * s.half : (which + 1) * s.half] = total(s, which).astype(BF)
        start(remote(out, pair, pair_sem.at[n], s.partner))

    out_t, out_p = y.at[pl.ds(0, 128)], x.at[pl.ds(0, P_ROWS)]
    unit_one(2)
    send_early(p1)
    unit_one(1)
    send_plain(p1, 0)
    unit_one(3)
    send_plain(p1, 1)
    send_early(p0)
    unit_one(0)
    send_joined(p1)
    send_plain(p0, 0)
    send_plain(p0, 1)
    unit_two(2)
    join_q(2)
    send_early(q0)
    join_q(1)
    send_plain(q0, 0)
    join_q(3)
    send_plain(q0, 1)
    for j, s in ((1, t1), (0, t0)):
        join_core(s, j, 2)
        send_early(s)
    unit_two(1)
    for j, s in ((1, t1), (0, t0)):
        join_core(s, j, 1)
        send_plain(s, 0)
    send_joined(p0)
    unit_two(3)
    for j, s in ((1, t1), (0, t0)):
        join_core(s, j, 3)
        send_plain(s, 1)
    send_joined(q0)
    to_pair(p1, out_p, pair_p, 0)
    unit_two(0)
    for j, s in ((1, t1), (0, t0)):
        join_core(s, j, 0)
        send_joined(s)
    join_q(0)
    to_pair(t1, out_t, pair_t, 1)
    for which in range(2):
        first = P_ROWS + which * q0.half
        slope[first : first + q0.half] = total(q0, which)
    done = pltpu.make_async_copy(slope.at[pl.ds(0, 128)], avg_two, local_sem.at[5])
    for s, out, pair, n in ((t0, out_t, pair_t, 1), (p0, out_p, pair_p, 0)):
        full = [total(s, which) for which in range(2)]
        remote(out, pair, pair_sem.at[n], twin).wait_recv()
        if n == 0:
            done.wait()
        for which in range(2):
            rows = slice(which * s.half, (which + 1) * s.half)
            slope[rows] = full[which] + pair[rows].astype(F32)
        if n == 1:
            done.start()
    done = pltpu.make_async_copy(slope, avg_one, local_sem.at[5])
    done.start()
    for copy in sent:
        copy.wait_send()
    done.wait()


def one_round(routes, counts, docs, targs, module_one, module_two):
    sem = pltpu.SemaphoreType.DMA
    v = lambda *shape: pltpu.VMEM(shape, BF)
    act = v(SLOTS, D)
    p, q = P_ROWS // 2, Q_ROWS // 2
    return pl.pallas_call(
        round_kernel,
        out_shape=(
            jax.ShapeDtypeStruct((2, PATHS, 8, D // 2), BF),
            jax.ShapeDtypeStruct((256, D), F32),
            jax.ShapeDtypeStruct((128, D), F32),
        ),
        in_specs=[VMEM] + [ANY] * 5,
        out_specs=(ANY, ANY, ANY),
        scratch_shapes=[pltpu.VMEM((N_ROW, N_COL), jnp.int32)]
        + [v(D, D)] * 4
        + [v(2, 32, 8, D // 2)]
        + [act] * 5
        + [pltpu.VMEM((SLOTS, D), F32)]
        + [v(D, SLOTS)] * 2
        + [v(2, 2, p, D), v(2, 2, 2, p, D), v(2 * p, D)]
        + [v(4, 2 * q, D), v(2, q, D), v(2, 2, q, D)]
        + [v(4, 2, 128, D), v(2, 2, 64, D), v(2, 2, 2, 64, D), v(128, D)]
        + [sem((5, 2, 2, 2)), sem((5, 2, 2)), sem((2, 2)), sem((4, 2)), sem((4, 2, 2)), sem((2, 2)), sem((8,))]
        + [sem((5, 2, 2)), sem((5, 2, 2, 2)), sem((2, 2)), sem((4, 2)), sem((4, 2, 2))],
        compiler_params=pltpu.CompilerParams(has_side_effects=True, vmem_limit_bytes=67043328),
        name="round",
    )(routes, counts, docs, targs, module_one, module_two)


def shards(documents, targets, routes, doc_counts, module_one, module_two, moment_one, moment_two):
    got, avg_one, avg_two = one_round(
        routes.reshape(2, 1, ROWS), doc_counts, documents, targets, module_one, module_two
    )
    next_moment_one = outer_moment * moment_one + avg_one[None]
    next_moment_two = outer_moment * moment_two + avg_two[None]
    new_one = module_one - outer_rate * (outer_moment * next_moment_one + avg_one[None])
    new_two = module_two - outer_rate * (outer_moment * next_moment_two + avg_two[None])
    return (new_one, new_two, next_moment_one, next_moment_two)


def solution(mesh):
    return jax.shard_map(
        shards,
        mesh=mesh,
        in_specs=(
            P(None, ("row", "col"), None),
            P(None, ("row", "col"), None),
            P(None, ("row", "col"), None),
            P(),
            P("row", "col", None),
            P("col", "row", None),
            P("row", "col", None),
            P("col", "row", None),
        ),
        out_specs=(
            P("row", "col", None),
            P("col", "row", None),
            P("row", "col", None),
            P("col", "row", None),
        ),
        check_vma=False,
    )
```

```python
import functools

import jax
import jax.numpy as jnp
from jax import lax
from jax.experimental import pallas as pl
from jax.experimental.pallas import tpu as pltpu
from jax.sharding import PartitionSpec as P

D = 2048
ROWS = 128
PATHS = 128
SLOTS = 256
N_ROW = 16
N_COL = 8
SCALE = D ** (-0.5)
GUARD = 0.5 / (D * ROWS) ** 0.5 / SCALE

outer_rate = 0.7
outer_moment = 0.9

BF = jnp.bfloat16
F32 = jnp.float32
MESH = pl.DeviceIdType.MESH
ANY = pl.BlockSpec(memory_space=pl.ANY)
VMEM = pl.BlockSpec(memory_space=pltpu.VMEM)


def iota(shape, dim):
    return lax.broadcasted_iota(jnp.int32, shape, dim)


P_GATHER = 160
P_ROWS = 160
Q_ROWS = 256 - P_ROWS


class Stream:
    def __init__(self, **fields):
        self.__dict__.update(fields)

    def at(self, full, step, first, count):
        return full.at[pl.ds(pl.multiple_of(self.rows((self.place + step) % 4) + first, 8), count)]


def remote(src, dst, sems, device):
    return pltpu.make_async_remote_copy(
        src_ref=src, dst_ref=dst, send_sem=sems.at[0], recv_sem=sems.at[1], device_id=device, device_id_type=MESH
    )


def round_kernel(
    routes, counts_in, docs, targs, module_one, module_two, got, avg_one, avg_two,
    counts,
    one, two, g_one, g_two, stage, x, y, hid, err, inn, slope, x_t, h_t,
    early_p, late_p, pair_p, y_q, early_q, late_q, core_in, early_t, late_t, pair_t,
    ring_sem, fwd_sem, y_sem, q_sem, core_sem, a2a_sem, local_sem,
    early_sem, late_sem, pair_sem, yq_sem, core_two_sem,
):
    row, col = lax.axis_index("row"), lax.axis_index("col")
    xx, low, core = row // 4, (row // 2) % 2, row % 2
    z, high = col // 2, col % 2
    me = row * N_COL + col

    def device(x=xx, low=low, core=core, z=z, high=high):
        return (x * 4 + low * 2 + core, z * 2 + high)

    twin = device(core=1 - core)
    ring_one = dict(place=z, plus=device(z=(z + 1) % 4), minus=device(z=(z + 3) % 4), partner=device(high=1 - high))
    ring_two = dict(place=xx, plus=device(x=(xx + 1) % 4), minus=device(x=(xx + 3) % 4), partner=device(low=1 - low))

    def rows_one(first, j):
        return lambda place: (place * 2 + (high + j) % 2) * 256 + first

    def rows_two(j, core=core):
        return lambda place: (place * 4 + ((low + j) % 2) * 2 + core) * 128

    def parts_one(rows):
        p = [Stream(n=j, half=rows // 2, rows=rows_one(0, j), **ring_one) for j in range(2)]
        q = [Stream(n=2, half=128 - rows // 2, rows=rows_one(rows, j), **ring_one) for j in range(2)]
        return p + q

    p0, p1, q0, q1 = parts_one(P_GATHER)
    t0 = Stream(n=3, half=64, rows=rows_two(0), **ring_two)
    t1 = Stream(n=4, half=64, rows=rows_two(1), **ring_two)
    u0 = Stream(half=64, rows=rows_two(0, 1 - core), **ring_two)
    u1 = Stream(half=64, rows=rows_two(1, 1 - core), **ring_two)
    sent = []

    def start(copy):
        copy.start()
        sent.append(copy)

    def whole(s, full, step):
        return s.at(full, step, 0, 2 * s.half)

    def spread(s, full):
        for way, to in ((0, s.plus), (1, s.minus)):
            for which in (0, 1) if way == 0 else (1, 0):
                ref = s.at(full, 0, which * s.half, s.half)
                start(remote(ref, ref, ring_sem.at[s.n, way, which], to))

    def arrived(s, full, way, which):
        ref = s.at(full, 3 if way == 0 else 1, which * s.half, s.half)
        remote(ref, ref, ring_sem.at[s.n, way, which], twin).wait_recv()

    def forward(s, full):
        for way, to in ((0, s.plus), (1, s.minus)):
            arrived(s, full, way, way)
            ref = s.at(full, 3 if way == 0 else 1, way * s.half, s.half)
            start(remote(ref, ref, fwd_sem.at[s.n, way], to))

    def rest(s, full):
        arrived(s, full, 0, 1)
        arrived(s, full, 1, 0)

    def forwarded(s, full):
        for way in range(2):
            ref = s.at(full, 2, way * s.half, s.half)
            remote(ref, ref, fwd_sem.at[s.n, way], twin).wait_recv()

    def q_across(step):
        ref = whole(q0, one, step)
        start(remote(ref, ref, q_sem.at[step], q0.partner))

    def to_twin(s, j, step):
        ref = whole(s, two, step)
        start(remote(ref, ref, core_sem.at[step, j], twin))

    def unpack(m):
        o, i = iota((256, 256), 0), iota((256, 256), 1)
        source = o % 64 // 2 * 8 + o // 128 * 4 + o % 2 * 2 + o // 64 % 2
        pick = jnp.where(i == source, 1.0, 0.0).astype(BF)
        loads = [
            pltpu.make_async_copy(got.at[m, pl.ds(b * 32, 32)], stage.at[b % 2], local_sem.at[5 + b % 2]) for b in range(4)
        ]
        loads[0].start()
        loads[1].start()
        for b in range(4):
            loads[b].wait()
            part = stage[b % 2].reshape(256, D // 2)
            rows = jnp.dot(pick, part, preferred_element_type=F32).astype(BF)
            for half in range(2):
                cols = slice(half * 1024, (half + 1) * 1024)
                x[b * 64 : (b + 1) * 64, cols] = rows[half * 64 : half * 64 + 64]
                y[b * 64 : (b + 1) * 64, cols] = rows[128 + half * 64 : 192 + half * 64]
            if b < 2:
                loads[b + 2].start()

    upper = pltpu.make_async_copy(module_one.at[0, pl.ds(0, 128)], slope.at[pl.ds(0, 128)], local_sem.at[0])
    lower = pltpu.make_async_copy(module_one.at[0, pl.ds(128, 128)], slope.at[pl.ds(0, 128)], local_sem.at[1])
    other = pltpu.make_async_copy(module_two.at[0], slope.at[pl.ds(128, 128)], local_sem.at[2])
    upper.start()
    other.start()
    loads = [
        pltpu.make_async_copy(source.at[m], to.at[pl.ds(m * ROWS, ROWS)], local_sem.at[3 + m * 2 + n])
        for m in range(2)
        for n, (source, to) in enumerate(((docs, x), (targs, y)))
    ]
    loads.append(pltpu.make_async_copy(counts_in, counts, local_sem.at[7]))
    for copy in loads:
        copy.start()
    upper.wait()
    p0.at(one, 0, 0, 128)[...] = slope[0:128].astype(BF)
    lower.start()
    other.wait()
    whole(t0, two, 0)[...] = slope[128:256].astype(BF)
    start(remote(whole(t0, two, 0), whole(t0, two, 0), y_sem.at[1], t0.partner))
    lower.wait()
    p0.at(one, 0, 128, 128)[...] = slope[0:128].astype(BF)
    start(remote(whole(p0, one, 0), whole(p0, one, 0), y_sem.at[0], p0.partner))
    spread(p0, one)
    spread(t0, two)
    spread(q0, one)
    q_across(0)
    to_twin(t0, 0, 0)
    for copy in loads:
        copy.wait()

    def pack(m):
        to = routes[m]
        same_place = iota((ROWS, ROWS), 0) == iota((ROWS, ROWS), 1)
        down = jnp.sum(jnp.where(same_place, to, 0), axis=1, keepdims=True)
        same = jnp.where(down == to, 1, 0)
        earlier = jnp.where(iota((ROWS, ROWS), 0) < iota((ROWS, ROWS), 1), same, 0)
        rank = jnp.sum(earlier, axis=0, keepdims=True)

        def block(b, carry):
            total = jnp.zeros((256, D // 2), F32)
            for kind, source in enumerate((x, y)):
                for half in range(2):
                    slot = to * 8 + (kind * 4 + half) + rank * 2 - b * 256
                    pick = jnp.where(iota((256, ROWS), 0) == slot, 1.0, 0.0).astype(BF)
                    part = source[m * ROWS : (m + 1) * ROWS, half * 1024 : (half + 1) * 1024]
                    total += jnp.dot(pick, part, preferred_element_type=F32)
            g_one[pl.ds(pl.multiple_of(b * 256, 256), 256), m * 1024 : (m + 1) * 1024] = total.astype(BF)
            return carry

        lax.fori_loop(0, 4, block, 0)

    def slot_rows(m, path):
        return g_one.at[pl.ds(pl.multiple_of(path * 8, 8), 8), pl.ds(m * 1024, 1024)]

    def send_slots(m):
        def send(step, carry):
            t = step * 53 % PATHS
            to = device(
                x=(xx + t % 4) % 4,
                low=(low + t // 4 % 2) % 2,
                high=(high + t // 8 % 2) % 2,
                z=(z + t // 16 % 4) % 4,
                core=(core + t // 64) % 2,
            )
            remote(slot_rows(m, to[0] * N_COL + to[1]), got.at[m, me], a2a_sem.at[m], to).start()
            return carry

        lax.fori_loop(1, PATHS, send, 0)

    def all_slots(m):
        ref = got.at[m, pl.ds(0, PATHS - 1)]
        return remote(ref, ref, a2a_sem.at[m], twin)

    own_slots = [pltpu.make_async_copy(slot_rows(m, me), got.at[m, me], local_sem.at[m]) for m in range(2)]
    for m in range(2):
        pack(m)
        own_slots[m].start()
        if m == 0:
            send_slots(0)
    remote(whole(p1, one, 0), whole(p1, one, 0), y_sem.at[0], twin).wait_recv()
    spread(p1, one)
    remote(whole(t1, two, 0), whole(t1, two, 0), y_sem.at[1], twin).wait_recv()
    spread(t1, two)
    to_twin(t1, 1, 0)
    forward(p0, one)
    forward(t0, two)
    forward(q0, one)
    forward(p1, one)
    forward(t1, two)
    rest(q0, one)
    q_across(1)
    q_across(3)
    for j, s in ((0, t0), (1, t1)):
        rest(s, two)
        to_twin(s, j, 1)
        to_twin(s, j, 3)
    forwarded(q0, one)
    q_across(2)
    for j, s in ((0, t0), (1, t1)):
        forwarded(s, two)
        to_twin(s, j, 2)
    for copy in own_slots:
        copy.wait()
    all_slots(0).wait_recv()
    unpack(0)
    for step in range(4):
        ref = whole(q1, one, step)
        remote(ref, ref, q_sem.at[step], twin).wait_recv()
        for j, s in ((0, u0), (1, u1)):
            ref = whole(s, two, step)
            remote(ref, ref, core_sem.at[step, j], twin).wait_recv()
    for s in (p0, p1):
        rest(s, one)
        forwarded(s, one)
    send_slots(1)

    def spans(n, tile):
        return pl.ds(pl.multiple_of(n * tile, tile), tile)

    def passes():
        wide = 1024

        def pre_tile(n, carry):
            cols = spans(n, wide)
            pre = jnp.dot(x[...], one[:, cols], preferred_element_type=F32) * SCALE
            sig = 1.0 / (1.0 + jnp.exp(-pre))
            hid[:, cols] = (pre * sig).astype(BF)
            slope[:, cols] = sig * (1.0 + pre * (1.0 - sig))
            return carry

        lax.fori_loop(0, D // wide, pre_tile, 0)

        def err_tile(n, carry):
            cols = spans(n, wide)
            out = jnp.dot(hid[...], two[:, cols], preferred_element_type=F32) * SCALE
            out = x[:, cols].astype(F32) + out
            err[:, cols] = ((out - y[:, cols].astype(F32)) / ROWS).astype(BF)
            return carry

        lax.fori_loop(0, D // wide, err_tile, 0)

        def inn_tile(n, carry):
            cols = spans(n, wide)
            back = lax.dot_general(err[...], two[cols, :], (((1,), (1,)), ((), ())), preferred_element_type=F32)
            inn[:, cols] = (back * SCALE * slope[:, cols]).astype(BF)
            return carry

        lax.fori_loop(0, D // wide, inn_tile, 0)

        def turn(n, carry):
            cols = spans(n, 256)
            x_t[cols, :] = x[:, cols].T
            h_t[cols, :] = hid[:, cols].T
            return carry

        lax.fori_loop(0, D // 256, turn, 0)

    def first_update(left, right, w, g):
        def step(n, carry):
            rows, cols = spans(n // 4, 1024), spans(n % 4, 512)
            grad = jnp.dot(left[rows, :], right[:, cols], preferred_element_type=F32)
            update = grad / (jnp.abs(grad) + GUARD)
            g[rows, cols] = grad.astype(BF)
            w[rows, cols] = (0.99 * w[rows, cols].astype(F32) - 0.1 * update).astype(BF)
            return carry

        lax.fori_loop(0, 8, step, 0)

    tally = counts[...].astype(F32)
    in_row = jnp.where(iota((N_COL, N_ROW), 1) == row, tally, 0.0)
    in_col = jnp.where(iota((N_COL, N_ROW), 0) == col, tally, 0.0)
    mine = jnp.where(iota((N_COL, N_ROW), 0) == col, in_row, 0.0)

    def grand(v):
        return jnp.sum(jnp.sum(v, axis=0, keepdims=True), axis=1, keepdims=True)

    share_one, share_two = grand(mine) / grand(in_row), grand(mine) / grand(in_col)
    root = (0.05 / 0.0975) ** 0.5

    def last_update(left, right, w, g, weight, first_row):
        part_w, part_a = weight * (1.0 / 0.99 - 0.99), weight * (0.1 / 0.99)
        part_b = weight * (0.1 * (0.1 / 0.19) / root)

        def step(n, carry):
            rows, cols = pl.ds(pl.multiple_of(first_row, 512), 512), spans(n, 512)
            grad = jnp.dot(left[rows, :], right[:, cols], preferred_element_type=F32)
            before = g[rows, cols].astype(F32)
            update_a = before / (jnp.abs(before) + GUARD)
            second = 0.95 * (before * before) + grad * grad
            update_b = (0.9 * before + grad) / (jnp.sqrt(second) + GUARD / root)
            g[rows, cols] = (
                part_w * w[rows, cols].astype(F32) + part_a * update_a + part_b * update_b
            ).astype(BF)
            return carry

        lax.fori_loop(0, 4, step, 0)

    passes()
    for copy in sent:
        copy.wait_send()
    sent.clear()
    first_update(h_t, err, two, g_two)
    for m in range(2):
        all_slots(m).wait_send()
    first_update(x_t, inn, one, g_one)
    all_slots(1).wait_recv()
    unpack(1)
    passes()

    p0, p1, q0, q1 = parts_one(P_ROWS)
    for s, full, early, late in (
        (p0, g_one, early_p.at[0], late_p.at[0]),
        (p1, g_one, early_p.at[1], late_p.at[1]),
        (q0, g_one, early_q, late_q),
        (t0, g_two, early_t.at[0], late_t.at[0]),
        (t1, g_two, early_t.at[1], late_t.at[1]),
    ):
        s.full, s.early, s.late = full, early, late

    def send_early(s):
        for way, to in ((0, s.plus), (1, s.minus)):
            src = s.at(s.full, 2, way * s.half, s.half)
            start(remote(src, s.early.at[way], early_sem.at[s.n, way], to))

    def send_plain(s, way):
        other = 1 - way
        src = s.at(s.full, 1 if way == 0 else 3, other * s.half, s.half)
        to = s.plus if way == 0 else s.minus
        start(remote(src, s.late.at[way, other], late_sem.at[s.n, way, other], to))

    def send_joined(s):
        for way, to in ((0, s.plus), (1, s.minus)):
            buf = s.early.at[way]
            remote(buf, buf, early_sem.at[s.n, way], twin).wait_recv()
            mine = s.at(s.full, 1 if way == 0 else 3, way * s.half, s.half)
            buf[...] = (mine[...].astype(F32) + buf[...].astype(F32)).astype(BF)
            start(remote(buf, s.late.at[way, way], late_sem.at[s.n, way, way], to))

    def total(s, which):
        for way in range(2):
            buf = s.late.at[way, which]
            remote(buf, buf, late_sem.at[s.n, way, which], twin).wait_recv()
        return (
            s.at(s.full, 0, which * s.half, s.half)[...].astype(F32)
            + s.late.at[0, which][...].astype(F32)
            + s.late.at[1, which][...].astype(F32)
        )

    def join_q(step):
        buf = y_q.at[step]
        remote(buf, buf, yq_sem.at[step], twin).wait_recv()
        mine = whole(q0, g_one, step)
        mine[...] = (mine[...].astype(F32) + buf[...].astype(F32)).astype(BF)

    def join_core(s, j, step):
        buf = core_in.at[step, j]
        remote(buf, buf, core_two_sem.at[step, j], twin).wait_recv()
        mine = whole(s, g_two, step)
        mine[...] = (mine[...].astype(F32) + buf[...].astype(F32)).astype(BF)

    def unit_one(step):
        last_update(x_t, inn, one, g_one, share_one, (z + step) % 4 * 512)
        start(remote(whole(q1, g_one, step), y_q.at[step], yq_sem.at[step], q1.partner))

    def unit_two(step):
        last_update(h_t, err, two, g_two, share_two, (xx + step) % 4 * 512)
        for j, s in ((1, u1), (0, u0)):
            start(remote(whole(s, g_two, step), core_in.at[step, j], core_two_sem.at[step, j], twin))

    def to_pair(s, out, pair, n):
        for which in range(2):
            out[which * s.half : (which + 1) * s.half] = total(s, which).astype(BF)
        start(remote(out, pair, pair_sem.at[n], s.partner))

    out_t, out_p = y.at[pl.ds(0, 128)], x.at[pl.ds(0, P_ROWS)]
    def joins(step):
        for j, s in ((1, t1), (0, t0)):
            join_core(s, j, step)

    unit_one(2)
    send_early(p1)
    unit_one(1)
    send_plain(p1, 0)
    unit_one(3)
    send_plain(p1, 1)
    send_early(p0)
    unit_two(2)
    send_joined(p1)
    send_plain(p0, 0)
    send_plain(p0, 1)
    unit_two(1)
    joins(2)
    send_early(t1)
    send_early(t0)
    join_q(2)
    send_early(q0)
    unit_one(0)
    joins(1)
    send_plain(t1, 0)
    send_plain(t0, 0)
    join_q(1)
    send_plain(q0, 0)
    unit_two(3)
    send_joined(p0)
    join_q(3)
    send_plain(q0, 1)
    unit_two(0)
    joins(3)
    send_plain(t1, 1)
    send_joined(t1)
    send_plain(t0, 1)
    send_joined(t0)
    to_pair(p1, out_p, pair_p, 0)
    joins(0)
    join_q(0)
    send_joined(q0)
    to_pair(t1, out_t, pair_t, 1)
    for which in range(2):
        first = P_ROWS + which * q0.half
        slope[first : first + q0.half] = total(q0, which)
    done = pltpu.make_async_copy(slope.at[pl.ds(0, 128)], avg_two, local_sem.at[5])
    for s, out, pair, n in ((t0, out_t, pair_t, 1), (p0, out_p, pair_p, 0)):
        full = [total(s, which) for which in range(2)]
        remote(out, pair, pair_sem.at[n], twin).wait_recv()
        if n == 0:
            done.wait()
        for which in range(2):
            rows = slice(which * s.half, (which + 1) * s.half)
            slope[rows] = full[which] + pair[rows].astype(F32)
        if n == 1:
            done.start()
    done = pltpu.make_async_copy(slope, avg_one, local_sem.at[5])
    done.start()
    for copy in sent:
        copy.wait_send()
    done.wait()


def one_round(routes, counts, docs, targs, module_one, module_two):
    sem = pltpu.SemaphoreType.DMA
    v = lambda *shape: pltpu.VMEM(shape, BF)
    act = v(SLOTS, D)
    p, q = P_ROWS // 2, Q_ROWS // 2
    return pl.pallas_call(
        round_kernel,
        out_shape=(
            jax.ShapeDtypeStruct((2, PATHS, 8, D // 2), BF),
            jax.ShapeDtypeStruct((256, D), F32),
            jax.ShapeDtypeStruct((128, D), F32),
        ),
        in_specs=[VMEM] + [ANY] * 5,
        out_specs=(ANY, ANY, ANY),
        scratch_shapes=[pltpu.VMEM((N_COL, N_ROW), jnp.int32)]
        + [v(D, D)] * 4
        + [v(2, 32, 8, D // 2)]
        + [act] * 5
        + [pltpu.VMEM((SLOTS, D), F32)]
        + [v(D, SLOTS)] * 2
        + [v(2, 2, p, D), v(2, 2, 2, p, D), v(2 * p, D)]
        + [v(4, 2 * q, D), v(2, q, D), v(2, 2, q, D)]
        + [v(4, 2, 128, D), v(2, 2, 64, D), v(2, 2, 2, 64, D), v(128, D)]
        + [sem((5, 2, 2, 2)), sem((5, 2, 2)), sem((2, 2)), sem((4, 2)), sem((4, 2, 2)), sem((2, 2)), sem((8,))]
        + [sem((5, 2, 2)), sem((5, 2, 2, 2)), sem((2, 2)), sem((4, 2)), sem((4, 2, 2))],
        compiler_params=pltpu.CompilerParams(has_side_effects=True, vmem_limit_bytes=67043328),
        name="round",
    )(routes, counts, docs, targs, module_one, module_two)


def shards(documents, targets, routes, doc_counts, module_one, module_two, moment_one, moment_two):
    got, avg_one, avg_two = one_round(
        routes.reshape(2, 1, ROWS), doc_counts.T, documents, targets, module_one, module_two
    )
    next_moment_one = outer_moment * moment_one + avg_one[None]
    next_moment_two = outer_moment * moment_two + avg_two[None]
    new_one = module_one - outer_rate * (outer_moment * next_moment_one + avg_one[None])
    new_two = module_two - outer_rate * (outer_moment * next_moment_two + avg_two[None])
    return (new_one, new_two, next_moment_one, next_moment_two)


def solution(mesh):
    return jax.shard_map(
        shards,
        mesh=mesh,
        in_specs=(
            P(None, ("row", "col"), None),
            P(None, ("row", "col"), None),
            P(None, ("row", "col"), None),
            P(),
            P("row", "col", None),
            P("col", "row", None),
            P("row", "col", None),
            P("col", "row", None),
        ),
        out_specs=(
            P("row", "col", None),
            P("col", "row", None),
            P("row", "col", None),
            P("col", "row", None),
        ),
        check_vma=False,
    )
```

```python
import functools

import jax
import jax.numpy as jnp
from jax import lax
from jax.experimental import pallas as pl
from jax.experimental.pallas import tpu as pltpu
from jax.sharding import PartitionSpec as P

D = 2048
ROWS = 128
PATHS = 128
SLOTS = 256
N_ROW = 16
N_COL = 8
SCALE = D ** (-0.5)
GUARD = 0.5 / (D * ROWS) ** 0.5 / SCALE

outer_rate = 0.7
outer_moment = 0.9

BF = jnp.bfloat16
F32 = jnp.float32
MESH = pl.DeviceIdType.MESH
ANY = pl.BlockSpec(memory_space=pl.ANY)
VMEM = pl.BlockSpec(memory_space=pltpu.VMEM)


def iota(shape, dim):
    return lax.broadcasted_iota(jnp.int32, shape, dim)


P_GATHER = 160
P_ROWS = 160
Q_ROWS = 256 - P_ROWS


class Stream:
    def __init__(self, **fields):
        self.__dict__.update(fields)

    def at(self, full, step, first, count):
        return full.at[pl.ds(pl.multiple_of(self.rows((self.place + step) % 4) + first, 8), count)]


def remote(src, dst, sems, device):
    return pltpu.make_async_remote_copy(
        src_ref=src, dst_ref=dst, send_sem=sems.at[0], recv_sem=sems.at[1], device_id=device, device_id_type=MESH
    )


def round_kernel(
    routes, counts_in, docs, targs, module_one, module_two, got, avg_one, avg_two,
    counts,
    one, two, g_one, g_two, stage, x, y, hid, err, inn, slope, x_t, h_t,
    early_p, late_p, pair_p, y_q, early_q, late_q, core_in, early_t, late_t, pair_t,
    ring_sem, fwd_sem, y_sem, q_sem, core_sem, a2a_sem, local_sem,
    early_sem, late_sem, pair_sem, yq_sem, core_two_sem,
):
    row, col = lax.axis_index("row"), lax.axis_index("col")
    xx, low, core = row // 4, (row // 2) % 2, row % 2
    z, high = col // 2, col % 2
    me = row * N_COL + col

    def device(x=xx, low=low, core=core, z=z, high=high):
        return (x * 4 + low * 2 + core, z * 2 + high)

    twin = device(core=1 - core)
    ring_one = dict(place=z, plus=device(z=(z + 1) % 4), minus=device(z=(z + 3) % 4), partner=device(high=1 - high))
    ring_two = dict(place=xx, plus=device(x=(xx + 1) % 4), minus=device(x=(xx + 3) % 4), partner=device(low=1 - low))

    def rows_one(first, j):
        return lambda place: (place * 2 + (high + j) % 2) * 256 + first

    def rows_two(j, core=core):
        return lambda place: (place * 4 + ((low + j) % 2) * 2 + core) * 128

    def parts_one(rows):
        p = [Stream(n=j, half=rows // 2, rows=rows_one(0, j), **ring_one) for j in range(2)]
        q = [Stream(n=2, half=128 - rows // 2, rows=rows_one(rows, j), **ring_one) for j in range(2)]
        return p + q

    p0, p1, q0, q1 = parts_one(P_GATHER)
    t0 = Stream(n=3, half=64, rows=rows_two(0), **ring_two)
    t1 = Stream(n=4, half=64, rows=rows_two(1), **ring_two)
    u0 = Stream(half=64, rows=rows_two(0, 1 - core), **ring_two)
    u1 = Stream(half=64, rows=rows_two(1, 1 - core), **ring_two)
    sent = []

    def start(copy):
        copy.start()
        sent.append(copy)

    def whole(s, full, step):
        return s.at(full, step, 0, 2 * s.half)

    def spread(s, full):
        for way, to in ((0, s.plus), (1, s.minus)):
            for which in (0, 1) if way == 0 else (1, 0):
                ref = s.at(full, 0, which * s.half, s.half)
                start(remote(ref, ref, ring_sem.at[s.n, way, which], to))

    def arrived(s, full, way, which):
        ref = s.at(full, 3 if way == 0 else 1, which * s.half, s.half)
        remote(ref, ref, ring_sem.at[s.n, way, which], twin).wait_recv()

    def forward(s, full):
        for way, to in ((0, s.plus), (1, s.minus)):
            arrived(s, full, way, way)
            ref = s.at(full, 3 if way == 0 else 1, way * s.half, s.half)
            start(remote(ref, ref, fwd_sem.at[s.n, way], to))

    def rest(s, full):
        arrived(s, full, 0, 1)
        arrived(s, full, 1, 0)

    def forwarded(s, full):
        for way in range(2):
            ref = s.at(full, 2, way * s.half, s.half)
            remote(ref, ref, fwd_sem.at[s.n, way], twin).wait_recv()

    def q_across(step):
        ref = whole(q0, one, step)
        start(remote(ref, ref, q_sem.at[step], q0.partner))

    def to_twin(s, j, step):
        ref = whole(s, two, step)
        start(remote(ref, ref, core_sem.at[step, j], twin))

    def unpack(m):
        o, i = iota((256, 256), 0), iota((256, 256), 1)
        source = o % 64 // 2 * 8 + o // 128 * 4 + o % 2 * 2 + o // 64 % 2
        pick = jnp.where(i == source, 1.0, 0.0).astype(BF)
        loads = [
            pltpu.make_async_copy(got.at[m, pl.ds(b * 32, 32)], stage.at[b % 2], local_sem.at[5 + b % 2]) for b in range(4)
        ]
        loads[0].start()
        loads[1].start()
        for b in range(4):
            loads[b].wait()
            part = stage[b % 2].reshape(256, D // 2)
            rows = jnp.dot(pick, part, preferred_element_type=F32).astype(BF)
            for half in range(2):
                cols = slice(half * 1024, (half + 1) * 1024)
                x[b * 64 : (b + 1) * 64, cols] = rows[half * 64 : half * 64 + 64]
                y[b * 64 : (b + 1) * 64, cols] = rows[128 + half * 64 : 192 + half * 64]
            if b < 2:
                loads[b + 2].start()

    barrier = pltpu.get_barrier_semaphore()

    def torus(t):
        return device(
            x=(xx + t % 4) % 4,
            low=(low + t // 4 % 2) % 2,
            high=(high + t // 8 % 2) % 2,
            z=(z + t // 16 % 4) % 4,
            core=(core + t // 64) % 2,
        )

    def greet(step, carry):
        pl.semaphore_signal(barrier, inc=1, device_id=torus(step), device_id_type=MESH)
        return carry

    upper = pltpu.make_async_copy(module_one.at[0, pl.ds(0, 128)], slope.at[pl.ds(0, 128)], local_sem.at[0])
    lower = pltpu.make_async_copy(module_one.at[0, pl.ds(128, 128)], slope.at[pl.ds(0, 128)], local_sem.at[1])
    other = pltpu.make_async_copy(module_two.at[0], slope.at[pl.ds(128, 128)], local_sem.at[2])
    upper.start()
    other.start()
    loads = [
        pltpu.make_async_copy(source.at[m], to.at[pl.ds(m * ROWS, ROWS)], local_sem.at[3 + m * 2 + n])
        for m in range(2)
        for n, (source, to) in enumerate(((docs, x), (targs, y)))
    ]
    loads.append(pltpu.make_async_copy(counts_in, counts, local_sem.at[7]))
    for copy in loads:
        copy.start()
    lax.fori_loop(1, PATHS, greet, 0)
    upper.wait()
    p0.at(one, 0, 0, 128)[...] = slope[0:128].astype(BF)
    lower.start()
    other.wait()
    whole(t0, two, 0)[...] = slope[128:256].astype(BF)
    lower.wait()
    p0.at(one, 0, 128, 128)[...] = slope[0:128].astype(BF)
    pl.semaphore_wait(barrier, PATHS - 1)
    start(remote(whole(p0, one, 0), whole(p0, one, 0), y_sem.at[0], p0.partner))
    start(remote(whole(t0, two, 0), whole(t0, two, 0), y_sem.at[1], t0.partner))
    spread(p0, one)
    spread(t0, two)
    spread(q0, one)
    q_across(0)
    to_twin(t0, 0, 0)
    for copy in loads:
        copy.wait()

    def pack(m):
        to = routes[m]
        same_place = iota((ROWS, ROWS), 0) == iota((ROWS, ROWS), 1)
        down = jnp.sum(jnp.where(same_place, to, 0), axis=1, keepdims=True)
        same = jnp.where(down == to, 1, 0)
        earlier = jnp.where(iota((ROWS, ROWS), 0) < iota((ROWS, ROWS), 1), same, 0)
        rank = jnp.sum(earlier, axis=0, keepdims=True)

        def block(b, carry):
            total = jnp.zeros((256, D // 2), F32)
            for kind, source in enumerate((x, y)):
                for half in range(2):
                    slot = to * 8 + (kind * 4 + half) + rank * 2 - b * 256
                    pick = jnp.where(iota((256, ROWS), 0) == slot, 1.0, 0.0).astype(BF)
                    part = source[m * ROWS : (m + 1) * ROWS, half * 1024 : (half + 1) * 1024]
                    total += jnp.dot(pick, part, preferred_element_type=F32)
            g_one[pl.ds(pl.multiple_of(b * 256, 256), 256), m * 1024 : (m + 1) * 1024] = total.astype(BF)
            return carry

        lax.fori_loop(0, 4, block, 0)

    def slot_rows(m, path):
        return g_one.at[pl.ds(pl.multiple_of(path * 8, 8), 8), pl.ds(m * 1024, 1024)]

    def send_slots(m):
        def send(step, carry):
            t = step * 53 % PATHS
            to = torus(t)
            remote(slot_rows(m, to[0] * N_COL + to[1]), got.at[m, me], a2a_sem.at[m], to).start()
            return carry

        lax.fori_loop(1, PATHS, send, 0)

    def all_slots(m):
        ref = got.at[m, pl.ds(0, PATHS - 1)]
        return remote(ref, ref, a2a_sem.at[m], twin)

    own_slots = [pltpu.make_async_copy(slot_rows(m, me), got.at[m, me], local_sem.at[m]) for m in range(2)]
    for m in range(2):
        pack(m)
        own_slots[m].start()
        if m == 0:
            send_slots(0)
    remote(whole(p1, one, 0), whole(p1, one, 0), y_sem.at[0], twin).wait_recv()
    spread(p1, one)
    remote(whole(t1, two, 0), whole(t1, two, 0), y_sem.at[1], twin).wait_recv()
    spread(t1, two)
    to_twin(t1, 1, 0)
    forward(p0, one)
    forward(t0, two)
    forward(q0, one)
    forward(p1, one)
    forward(t1, two)
    rest(q0, one)
    q_across(1)
    q_across(3)
    for j, s in ((0, t0), (1, t1)):
        rest(s, two)
        to_twin(s, j, 1)
        to_twin(s, j, 3)
    forwarded(q0, one)
    q_across(2)
    for j, s in ((0, t0), (1, t1)):
        forwarded(s, two)
        to_twin(s, j, 2)
    for copy in own_slots:
        copy.wait()
    all_slots(0).wait_recv()
    unpack(0)
    for step in range(4):
        ref = whole(q1, one, step)
        remote(ref, ref, q_sem.at[step], twin).wait_recv()
        for j, s in ((0, u0), (1, u1)):
            ref = whole(s, two, step)
            remote(ref, ref, core_sem.at[step, j], twin).wait_recv()
    for s in (p0, p1):
        rest(s, one)
        forwarded(s, one)
    send_slots(1)

    def spans(n, tile):
        return pl.ds(pl.multiple_of(n * tile, tile), tile)

    def passes():
        wide = 1024

        def pre_tile(n, carry):
            cols = spans(n, wide)
            pre = jnp.dot(x[...], one[:, cols], preferred_element_type=F32) * SCALE
            sig = 1.0 / (1.0 + jnp.exp(-pre))
            hid[:, cols] = (pre * sig).astype(BF)
            slope[:, cols] = sig * (1.0 + pre * (1.0 - sig))
            return carry

        lax.fori_loop(0, D // wide, pre_tile, 0)

        def err_tile(n, carry):
            cols = spans(n, wide)
            out = jnp.dot(hid[...], two[:, cols], preferred_element_type=F32) * SCALE
            out = x[:, cols].astype(F32) + out
            err[:, cols] = ((out - y[:, cols].astype(F32)) / ROWS).astype(BF)
            return carry

        lax.fori_loop(0, D // wide, err_tile, 0)

        def inn_tile(n, carry):
            cols = spans(n, wide)
            back = lax.dot_general(err[...], two[cols, :], (((1,), (1,)), ((), ())), preferred_element_type=F32)
            inn[:, cols] = (back * SCALE * slope[:, cols]).astype(BF)
            return carry

        lax.fori_loop(0, D // wide, inn_tile, 0)

        def turn(n, carry):
            cols = spans(n, 256)
            x_t[cols, :] = x[:, cols].T
            h_t[cols, :] = hid[:, cols].T
            return carry

        lax.fori_loop(0, D // 256, turn, 0)

    def first_update(left, right, w, g):
        def step(n, carry):
            rows, cols = spans(n // 4, 1024), spans(n % 4, 512)
            grad = jnp.dot(left[rows, :], right[:, cols], preferred_element_type=F32)
            update = grad / (jnp.abs(grad) + GUARD)
            g[rows, cols] = grad.astype(BF)
            w[rows, cols] = (0.99 * w[rows, cols].astype(F32) - 0.1 * update).astype(BF)
            return carry

        lax.fori_loop(0, 8, step, 0)

    tally = counts[...].astype(F32)
    in_row = jnp.where(iota((N_COL, N_ROW), 1) == row, tally, 0.0)
    in_col = jnp.where(iota((N_COL, N_ROW), 0) == col, tally, 0.0)
    mine = jnp.where(iota((N_COL, N_ROW), 0) == col, in_row, 0.0)

    def grand(v):
        return jnp.sum(jnp.sum(v, axis=0, keepdims=True), axis=1, keepdims=True)

    share_one, share_two = grand(mine) / grand(in_row), grand(mine) / grand(in_col)
    root = (0.05 / 0.0975) ** 0.5

    def last_update(left, right, w, g, weight, first_row):
        part_w, part_a = weight * (1.0 / 0.99 - 0.99), weight * (0.1 / 0.99)
        part_b = weight * (0.1 * (0.1 / 0.19) / root)

        def step(n, carry):
            rows, cols = pl.ds(pl.multiple_of(first_row, 512), 512), spans(n, 512)
            grad = jnp.dot(left[rows, :], right[:, cols], preferred_element_type=F32)
            before = g[rows, cols].astype(F32)
            update_a = before / (jnp.abs(before) + GUARD)
            second = 0.95 * (before * before) + grad * grad
            update_b = (0.9 * before + grad) / (jnp.sqrt(second) + GUARD / root)
            g[rows, cols] = (
                part_w * w[rows, cols].astype(F32) + part_a * update_a + part_b * update_b
            ).astype(BF)
            return carry

        lax.fori_loop(0, 4, step, 0)

    passes()
    for copy in sent:
        copy.wait_send()
    sent.clear()
    first_update(h_t, err, two, g_two)
    for m in range(2):
        all_slots(m).wait_send()
    first_update(x_t, inn, one, g_one)
    all_slots(1).wait_recv()
    unpack(1)
    passes()

    p0, p1, q0, q1 = parts_one(P_ROWS)
    for s, full, early, late in (
        (p0, g_one, early_p.at[0], late_p.at[0]),
        (p1, g_one, early_p.at[1], late_p.at[1]),
        (q0, g_one, early_q, late_q),
        (t0, g_two, early_t.at[0], late_t.at[0]),
        (t1, g_two, early_t.at[1], late_t.at[1]),
    ):
        s.full, s.early, s.late = full, early, late

    def send_early(s):
        for way, to in ((0, s.plus), (1, s.minus)):
            src = s.at(s.full, 2, way * s.half, s.half)
            start(remote(src, s.early.at[way], early_sem.at[s.n, way], to))

    def send_plain(s, way):
        other = 1 - way
        src = s.at(s.full, 1 if way == 0 else 3, other * s.half, s.half)
        to = s.plus if way == 0 else s.minus
        start(remote(src, s.late.at[way, other], late_sem.at[s.n, way, other], to))

    def send_joined(s):
        for way, to in ((0, s.plus), (1, s.minus)):
            buf = s.early.at[way]
            remote(buf, buf, early_sem.at[s.n, way], twin).wait_recv()
            mine = s.at(s.full, 1 if way == 0 else 3, way * s.half, s.half)
            buf[...] = (mine[...].astype(F32) + buf[...].astype(F32)).astype(BF)
            start(remote(buf, s.late.at[way, way], late_sem.at[s.n, way, way], to))

    def total(s, which):
        for way in range(2):
            buf = s.late.at[way, which]
            remote(buf, buf, late_sem.at[s.n, way, which], twin).wait_recv()
        return (
            s.at(s.full, 0, which * s.half, s.half)[...].astype(F32)
            + s.late.at[0, which][...].astype(F32)
            + s.late.at[1, which][...].astype(F32)
        )

    def join_q(step):
        buf = y_q.at[step]
        remote(buf, buf, yq_sem.at[step], twin).wait_recv()
        mine = whole(q0, g_one, step)
        mine[...] = (mine[...].astype(F32) + buf[...].astype(F32)).astype(BF)

    def join_core(s, j, step):
        buf = core_in.at[step, j]
        remote(buf, buf, core_two_sem.at[step, j], twin).wait_recv()
        mine = whole(s, g_two, step)
        mine[...] = (mine[...].astype(F32) + buf[...].astype(F32)).astype(BF)

    def unit_one(step):
        last_update(x_t, inn, one, g_one, share_one, (z + step) % 4 * 512)
        start(remote(whole(q1, g_one, step), y_q.at[step], yq_sem.at[step], q1.partner))

    def unit_two(step):
        last_update(h_t, err, two, g_two, share_two, (xx + step) % 4 * 512)
        for j, s in ((1, u1), (0, u0)):
            start(remote(whole(s, g_two, step), core_in.at[step, j], core_two_sem.at[step, j], twin))

    def to_pair(s, out, pair, n):
        for which in range(2):
            out[which * s.half : (which + 1) * s.half] = total(s, which).astype(BF)
        start(remote(out, pair, pair_sem.at[n], s.partner))

    out_t, out_p = y.at[pl.ds(0, 128)], x.at[pl.ds(0, P_ROWS)]
    def joins(step):
        for j, s in ((1, t1), (0, t0)):
            join_core(s, j, step)

    unit_one(2)
    send_early(p1)
    unit_one(1)
    send_plain(p1, 0)
    unit_one(3)
    send_plain(p1, 1)
    send_early(p0)
    unit_two(2)
    send_joined(p1)
    send_plain(p0, 0)
    send_plain(p0, 1)
    unit_two(1)
    joins(2)
    send_early(t1)
    send_early(t0)
    join_q(2)
    send_early(q0)
    unit_one(0)
    joins(1)
    send_plain(t1, 0)
    send_plain(t0, 0)
    join_q(1)
    send_plain(q0, 0)
    unit_two(3)
    send_joined(p0)
    join_q(3)
    send_plain(q0, 1)
    unit_two(0)
    joins(3)
    send_plain(t1, 1)
    send_joined(t1)
    send_plain(t0, 1)
    send_joined(t0)
    to_pair(p1, out_p, pair_p, 0)
    joins(0)
    join_q(0)
    send_joined(q0)
    to_pair(t1, out_t, pair_t, 1)
    for which in range(2):
        first = P_ROWS + which * q0.half
        slope[first : first + q0.half] = total(q0, which)
    done = pltpu.make_async_copy(slope.at[pl.ds(0, 128)], avg_two, local_sem.at[5])
    for s, out, pair, n in ((t0, out_t, pair_t, 1), (p0, out_p, pair_p, 0)):
        full = [total(s, which) for which in range(2)]
        remote(out, pair, pair_sem.at[n], twin).wait_recv()
        if n == 0:
            done.wait()
        for which in range(2):
            rows = slice(which * s.half, (which + 1) * s.half)
            slope[rows] = full[which] + pair[rows].astype(F32)
        if n == 1:
            done.start()
    done = pltpu.make_async_copy(slope, avg_one, local_sem.at[5])
    done.start()
    for copy in sent:
        copy.wait_send()
    done.wait()


def one_round(routes, counts, docs, targs, module_one, module_two):
    sem = pltpu.SemaphoreType.DMA
    v = lambda *shape: pltpu.VMEM(shape, BF)
    act = v(SLOTS, D)
    p, q = P_ROWS // 2, Q_ROWS // 2
    return pl.pallas_call(
        round_kernel,
        out_shape=(
            jax.ShapeDtypeStruct((2, PATHS, 8, D // 2), BF),
            jax.ShapeDtypeStruct((256, D), F32),
            jax.ShapeDtypeStruct((128, D), F32),
        ),
        in_specs=[VMEM] + [ANY] * 5,
        out_specs=(ANY, ANY, ANY),
        scratch_shapes=[pltpu.VMEM((N_COL, N_ROW), jnp.int32)]
        + [v(D, D)] * 4
        + [v(2, 32, 8, D // 2)]
        + [act] * 5
        + [pltpu.VMEM((SLOTS, D), F32)]
        + [v(D, SLOTS)] * 2
        + [v(2, 2, p, D), v(2, 2, 2, p, D), v(2 * p, D)]
        + [v(4, 2 * q, D), v(2, q, D), v(2, 2, q, D)]
        + [v(4, 2, 128, D), v(2, 2, 64, D), v(2, 2, 2, 64, D), v(128, D)]
        + [sem((5, 2, 2, 2)), sem((5, 2, 2)), sem((2, 2)), sem((4, 2)), sem((4, 2, 2)), sem((2, 2)), sem((8,))]
        + [sem((5, 2, 2)), sem((5, 2, 2, 2)), sem((2, 2)), sem((4, 2)), sem((4, 2, 2))],
        compiler_params=pltpu.CompilerParams(has_side_effects=True, collective_id=0, vmem_limit_bytes=67043328),
        name="round",
    )(routes, counts, docs, targs, module_one, module_two)


def shards(documents, targets, routes, doc_counts, module_one, module_two, moment_one, moment_two):
    got, avg_one, avg_two = one_round(
        routes.reshape(2, 1, ROWS), doc_counts.T, documents, targets, module_one, module_two
    )
    next_moment_one = outer_moment * moment_one + avg_one[None]
    next_moment_two = outer_moment * moment_two + avg_two[None]
    new_one = module_one - outer_rate * (outer_moment * next_moment_one + avg_one[None])
    new_two = module_two - outer_rate * (outer_moment * next_moment_two + avg_two[None])
    return (new_one, new_two, next_moment_one, next_moment_two)


def solution(mesh):
    return jax.shard_map(
        shards,
        mesh=mesh,
        in_specs=(
            P(None, ("row", "col"), None),
            P(None, ("row", "col"), None),
            P(None, ("row", "col"), None),
            P(),
            P("row", "col", None),
            P("col", "row", None),
            P("row", "col", None),
            P("col", "row", None),
        ),
        out_specs=(
            P("row", "col", None),
            P("col", "row", None),
            P("row", "col", None),
            P("col", "row", None),
        ),
        check_vma=False,
    )
```

```python
import functools

import jax
import jax.numpy as jnp
from jax import lax
from jax.experimental import pallas as pl
from jax.experimental.pallas import tpu as pltpu
from jax.sharding import PartitionSpec as P

D = 2048
ROWS = 128
PATHS = 128
SLOTS = 256
N_ROW = 16
N_COL = 8
SCALE = D ** (-0.5)
GUARD = 0.5 / (D * ROWS) ** 0.5 / SCALE

outer_rate = 0.7
outer_moment = 0.9

BF = jnp.bfloat16
F32 = jnp.float32
MESH = pl.DeviceIdType.MESH
ANY = pl.BlockSpec(memory_space=pl.ANY)
VMEM = pl.BlockSpec(memory_space=pltpu.VMEM)


def iota(shape, dim):
    return lax.broadcasted_iota(jnp.int32, shape, dim)


P_GATHER = 160
P_ROWS = 160
Q_ROWS = 256 - P_ROWS


class Stream:
    def __init__(self, **fields):
        self.__dict__.update(fields)

    def at(self, full, step, first, count):
        return full.at[pl.ds(pl.multiple_of(self.rows((self.place + step) % 4) + first, 8), count)]


def remote(src, dst, sems, device):
    return pltpu.make_async_remote_copy(
        src_ref=src, dst_ref=dst, send_sem=sems.at[0], recv_sem=sems.at[1], device_id=device, device_id_type=MESH
    )


def round_kernel(
    routes, counts_in, docs, targs, module_one, module_two, got, packed, avg_one, avg_two,
    counts,
    one, two, g_one, g_two, stage, x, y, hid, err, inn, slope, x_t, h_t,
    early_p, late_p, pair_p, y_q, early_q, late_q, core_in, early_t, late_t, pair_t,
    ring_sem, fwd_sem, y_sem, q_sem, core_sem, a2a_sem, local_sem,
    early_sem, late_sem, pair_sem, yq_sem, core_two_sem, pack_sem, own_sem,
):
    row, col = lax.axis_index("row"), lax.axis_index("col")
    xx, low, core = row // 4, (row // 2) % 2, row % 2
    z, high = col // 2, col % 2
    me = row * N_COL + col

    def device(x=xx, low=low, core=core, z=z, high=high):
        return (x * 4 + low * 2 + core, z * 2 + high)

    twin = device(core=1 - core)
    ring_one = dict(place=z, plus=device(z=(z + 1) % 4), minus=device(z=(z + 3) % 4), partner=device(high=1 - high))
    ring_two = dict(place=xx, plus=device(x=(xx + 1) % 4), minus=device(x=(xx + 3) % 4), partner=device(low=1 - low))

    def rows_one(first, j):
        return lambda place: (place * 2 + (high + j) % 2) * 256 + first

    def rows_two(j, core=core):
        return lambda place: (place * 4 + ((low + j) % 2) * 2 + core) * 128

    def parts_one(rows):
        p = [Stream(n=j, half=rows // 2, rows=rows_one(0, j), **ring_one) for j in range(2)]
        q = [Stream(n=2, half=128 - rows // 2, rows=rows_one(rows, j), **ring_one) for j in range(2)]
        return p + q

    p0, p1, q0, q1 = parts_one(P_GATHER)
    t0 = Stream(n=3, half=64, rows=rows_two(0), **ring_two)
    t1 = Stream(n=4, half=64, rows=rows_two(1), **ring_two)
    u0 = Stream(half=64, rows=rows_two(0, 1 - core), **ring_two)
    u1 = Stream(half=64, rows=rows_two(1, 1 - core), **ring_two)
    sent = []

    def start(copy):
        copy.start()
        sent.append(copy)

    def whole(s, full, step):
        return s.at(full, step, 0, 2 * s.half)

    def spread(s, full):
        for way, to in ((0, s.plus), (1, s.minus)):
            for which in (0, 1) if way == 0 else (1, 0):
                ref = s.at(full, 0, which * s.half, s.half)
                start(remote(ref, ref, ring_sem.at[s.n, way, which], to))

    def arrived(s, full, way, which):
        ref = s.at(full, 3 if way == 0 else 1, which * s.half, s.half)
        remote(ref, ref, ring_sem.at[s.n, way, which], twin).wait_recv()

    def forward(s, full):
        for way, to in ((0, s.plus), (1, s.minus)):
            arrived(s, full, way, way)
            ref = s.at(full, 3 if way == 0 else 1, way * s.half, s.half)
            start(remote(ref, ref, fwd_sem.at[s.n, way], to))

    def rest(s, full):
        arrived(s, full, 0, 1)
        arrived(s, full, 1, 0)

    def forwarded(s, full):
        for way in range(2):
            ref = s.at(full, 2, way * s.half, s.half)
            remote(ref, ref, fwd_sem.at[s.n, way], twin).wait_recv()

    def q_across(step):
        ref = whole(q0, one, step)
        start(remote(ref, ref, q_sem.at[step], q0.partner))

    def to_twin(s, j, step):
        ref = whole(s, two, step)
        start(remote(ref, ref, core_sem.at[step, j], twin))

    def unpack(ch, into):
        o, i = iota((256, 256), 0), iota((256, 256), 1)
        source = o % 64 // 2 * 8 + o % 2 * 4 + o // 64
        pick = jnp.where(i == source, 1.0, 0.0).astype(BF)
        loads = [
            pltpu.make_async_copy(got.at[ch, pl.ds(b * 32, 32)], stage.at[b], local_sem.at[b]) for b in range(4)
        ]
        for copy in loads:
            copy.start()
        for b in range(4):
            loads[b].wait()
            rows = jnp.dot(pick, stage[b].reshape(256, 512), preferred_element_type=F32).astype(BF)
            for quarter in range(4):
                cols = slice(quarter * 512, (quarter + 1) * 512)
                into[b * 64 : (b + 1) * 64, cols] = rows[quarter * 64 : (quarter + 1) * 64]

    barrier = pltpu.get_barrier_semaphore()

    def greet(step, carry):
        for n in range(8):
            to = device(
                x=(xx + n % 4) % 4,
                low=(low + n // 4) % 2,
                high=(high + step % 2) % 2,
                z=(z + step // 2 % 4) % 4,
                core=(core + step // 8) % 2,
            )
            pl.semaphore_signal(barrier, inc=1, device_id=to, device_id_type=MESH)
        return carry

    upper = pltpu.make_async_copy(module_one.at[0, pl.ds(0, 128)], slope.at[pl.ds(0, 128)], local_sem.at[0])
    lower = pltpu.make_async_copy(module_one.at[0, pl.ds(128, 128)], slope.at[pl.ds(0, 128)], local_sem.at[1])
    other = pltpu.make_async_copy(module_two.at[0], slope.at[pl.ds(128, 128)], local_sem.at[2])
    upper.start()
    other.start()
    loads = [
        pltpu.make_async_copy(source.at[m], to.at[pl.ds(m * ROWS, ROWS)], local_sem.at[3 + m * 2 + n])
        for m in range(2)
        for n, (source, to) in enumerate(((docs, x), (targs, y)))
    ]
    loads.append(pltpu.make_async_copy(counts_in, counts, local_sem.at[7]))
    for copy in loads:
        copy.start()
    for n in range(1, 8):
        to = device(x=(xx + n % 4) % 4, low=(low + n // 4) % 2)
        pl.semaphore_signal(barrier, inc=1, device_id=to, device_id_type=MESH)
    lax.fori_loop(1, 16, greet, 0)
    upper.wait()
    p0.at(one, 0, 0, 128)[...] = slope[0:128].astype(BF)
    lower.start()
    other.wait()
    whole(t0, two, 0)[...] = slope[128:256].astype(BF)
    lower.wait()
    p0.at(one, 0, 128, 128)[...] = slope[0:128].astype(BF)
    pl.semaphore_wait(barrier, PATHS - 1)
    start(remote(whole(p0, one, 0), whole(p0, one, 0), y_sem.at[0], p0.partner))
    start(remote(whole(t0, two, 0), whole(t0, two, 0), y_sem.at[1], t0.partner))
    spread(p0, one)
    spread(t0, two)
    spread(q0, one)
    q_across(0)
    to_twin(t0, 0, 0)
    for copy in loads:
        copy.wait()

    def pack(m):
        to = routes[m]
        same_place = iota((ROWS, ROWS), 0) == iota((ROWS, ROWS), 1)
        down = jnp.sum(jnp.where(same_place, to, 0), axis=1, keepdims=True)
        same = jnp.where(down == to, 1, 0)
        earlier = jnp.where(iota((ROWS, ROWS), 0) < iota((ROWS, ROWS), 1), same, 0)
        rank = jnp.sum(earlier, axis=0, keepdims=True)

        def block(b, carry):
            for kind, source in enumerate((x, y)):
                total = jnp.zeros((256, 512), F32)
                for quarter in range(4):
                    slot = to * 8 + rank * 4 + quarter - b * 256
                    pick = jnp.where(iota((256, ROWS), 0) == slot, 1.0, 0.0).astype(BF)
                    part = source[m * ROWS : (m + 1) * ROWS, quarter * 512 : (quarter + 1) * 512]
                    total += jnp.dot(pick, part, preferred_element_type=F32)
                rows = pl.ds(pl.multiple_of(b * 256, 256), 256)
                g_one[rows, (m * 2 + kind) * 512 : (m * 2 + kind + 1) * 512] = total.astype(BF)
            return carry

        lax.fori_loop(0, 4, block, 0)
        for kind in range(2):
            pltpu.make_async_copy(packed_part(m * 2 + kind), packed.at[m * 2 + kind], pack_sem.at[m * 2 + kind]).start()
        for kind in range(2):
            pltpu.make_async_copy(packed_part(m * 2 + kind), packed.at[m * 2 + kind], pack_sem.at[m * 2 + kind]).wait()

    def packed_part(ch):
        return g_one.at[pl.ds(0, PATHS * 8), pl.ds(ch * 512, 512)]

    def slot_rows(m, path):
        return packed.at[m, pl.ds(pl.multiple_of(path * 8, 8), 8)]

    row_of = [(xx + n % 4) % 4 * 4 + (low + n // 4) % 2 * 2 for n in range(8)]

    def send_slots(m):
        def send(turn, n):
            t = n * 53 % PATHS
            u = lax.rem(turn * 5 + t // 8, 16)
            to_high = lax.rem(high + lax.rem(u, 2), 2)
            to_z = lax.rem(z + lax.rem(lax.div(u, 2), 4), 4)
            to_core = lax.rem(core + lax.div(u, 8), 2)
            to = (row_of[t % 8] + to_core, to_z * 2 + to_high)
            remote(slot_rows(m, to[0] * N_COL + to[1]), got.at[m, me], a2a_sem.at[m], to).start()

        def eight(turn, carry):
            for n in range(8):
                send(turn, n)
            return carry

        for n in range(1, 8):
            send(jnp.int32(0), n)
        lax.fori_loop(1, 16, eight, 0)

    def all_slots(m):
        ref = got.at[m, pl.ds(0, PATHS - 1)]
        return remote(ref, ref, a2a_sem.at[m], twin)

    own_slots = [pltpu.make_async_copy(slot_rows(ch, me), got.at[ch, me], own_sem.at[ch]) for ch in range(4)]
    for m in range(2):
        pack(m)
        for kind in range(2):
            own_slots[m * 2 + kind].start()
            if m == 0:
                send_slots(kind)
    remote(whole(p1, one, 0), whole(p1, one, 0), y_sem.at[0], twin).wait_recv()
    spread(p1, one)
    remote(whole(t1, two, 0), whole(t1, two, 0), y_sem.at[1], twin).wait_recv()
    spread(t1, two)
    to_twin(t1, 1, 0)
    forward(p0, one)
    forward(t0, two)
    forward(q0, one)
    forward(p1, one)
    forward(t1, two)
    rest(q0, one)
    q_across(1)
    q_across(3)
    for j, s in ((0, t0), (1, t1)):
        rest(s, two)
        to_twin(s, j, 1)
        to_twin(s, j, 3)
    forwarded(q0, one)
    q_across(2)
    for j, s in ((0, t0), (1, t1)):
        forwarded(s, two)
        to_twin(s, j, 2)
    for copy in own_slots:
        copy.wait()
    all_slots(0).wait_recv()
    unpack(0, x)
    all_slots(1).wait_recv()
    unpack(1, y)
    for step in range(4):
        ref = whole(q1, one, step)
        remote(ref, ref, q_sem.at[step], twin).wait_recv()
        for j, s in ((0, u0), (1, u1)):
            ref = whole(s, two, step)
            remote(ref, ref, core_sem.at[step, j], twin).wait_recv()
    for s in (p0, p1):
        rest(s, one)
        forwarded(s, one)
    send_slots(2)

    def spans(n, tile):
        return pl.ds(pl.multiple_of(n * tile, tile), tile)

    wide = 1024

    def pre_pass():
        def pre_tile(n, carry):
            cols = spans(n, wide)
            pre = jnp.dot(x[...], one[:, cols], preferred_element_type=F32) * SCALE
            sig = 1.0 / (1.0 + jnp.exp(-pre))
            hid[:, cols] = (pre * sig).astype(BF)
            slope[:, cols] = sig * (1.0 + pre * (1.0 - sig))
            return carry

        lax.fori_loop(0, D // wide, pre_tile, 0)

    def err_pass():
        def err_tile(n, carry):
            cols = spans(n, wide)
            out = jnp.dot(hid[...], two[:, cols], preferred_element_type=F32) * SCALE
            out = x[:, cols].astype(F32) + out
            err[:, cols] = ((out - y[:, cols].astype(F32)) / ROWS).astype(BF)
            return carry

        lax.fori_loop(0, D // wide, err_tile, 0)

        def inn_tile(n, carry):
            cols = spans(n, wide)
            back = lax.dot_general(err[...], two[cols, :], (((1,), (1,)), ((), ())), preferred_element_type=F32)
            inn[:, cols] = (back * SCALE * slope[:, cols]).astype(BF)
            return carry

        lax.fori_loop(0, D // wide, inn_tile, 0)

    def turns():
        def turn(n, carry):
            cols = spans(n, 256)
            x_t[cols, :] = x[:, cols].T
            h_t[cols, :] = hid[:, cols].T
            return carry

        lax.fori_loop(0, D // 256, turn, 0)

    def first_update(left, right, w, g):
        def step(n, carry):
            rows, cols = spans(n // 4, 1024), spans(n % 4, 512)
            grad = jnp.dot(left[rows, :], right[:, cols], preferred_element_type=F32)
            update = grad / (jnp.abs(grad) + GUARD)
            g[rows, cols] = grad.astype(BF)
            w[rows, cols] = (0.99 * w[rows, cols].astype(F32) - 0.1 * update).astype(BF)
            return carry

        lax.fori_loop(0, 8, step, 0)

    tally = counts[...].astype(F32)
    in_row = jnp.where(iota((N_COL, N_ROW), 1) == row, tally, 0.0)
    in_col = jnp.where(iota((N_COL, N_ROW), 0) == col, tally, 0.0)
    mine = jnp.where(iota((N_COL, N_ROW), 0) == col, in_row, 0.0)

    def grand(v):
        return jnp.sum(jnp.sum(v, axis=0, keepdims=True), axis=1, keepdims=True)

    share_one, share_two = grand(mine) / grand(in_row), grand(mine) / grand(in_col)
    root = (0.05 / 0.0975) ** 0.5

    def last_update(left, right, w, g, weight, first_row):
        part_w, part_a = weight * (1.0 / 0.99 - 0.99), weight * (0.1 / 0.99)
        part_b = weight * (0.1 * (0.1 / 0.19) / root)

        def step(n, carry):
            rows, cols = pl.ds(pl.multiple_of(first_row, 512), 512), spans(n, 512)
            grad = jnp.dot(left[rows, :], right[:, cols], preferred_element_type=F32)
            before = g[rows, cols].astype(F32)
            update_a = before / (jnp.abs(before) + GUARD)
            second = 0.95 * (before * before) + grad * grad
            update_b = (0.9 * before + grad) / (jnp.sqrt(second) + GUARD / root)
            g[rows, cols] = (
                part_w * w[rows, cols].astype(F32) + part_a * update_a + part_b * update_b
            ).astype(BF)
            return carry

        lax.fori_loop(0, 4, step, 0)

    pre_pass()
    err_pass()
    turns()
    send_slots(3)
    for copy in sent:
        copy.wait_send()
    sent.clear()
    first_update(x_t, inn, one, g_one)
    all_slots(2).wait_recv()
    unpack(2, x)
    pre_pass()
    first_update(h_t, err, two, g_two)
    turns()
    all_slots(3).wait_recv()
    unpack(3, y)
    err_pass()
    for ch in range(4):
        all_slots(ch).wait_send()

    p0, p1, q0, q1 = parts_one(P_ROWS)
    for s, full, early, late in (
        (p0, g_one, early_p.at[0], late_p.at[0]),
        (p1, g_one, early_p.at[1], late_p.at[1]),
        (q0, g_one, early_q, late_q),
        (t0, g_two, early_t.at[0], late_t.at[0]),
        (t1, g_two, early_t.at[1], late_t.at[1]),
    ):
        s.full, s.early, s.late = full, early, late

    def send_early(s):
        for way, to in ((0, s.plus), (1, s.minus)):
            src = s.at(s.full, 2, way * s.half, s.half)
            start(remote(src, s.early.at[way], early_sem.at[s.n, way], to))

    def send_plain(s, way):
        other = 1 - way
        src = s.at(s.full, 1 if way == 0 else 3, other * s.half, s.half)
        to = s.plus if way == 0 else s.minus
        start(remote(src, s.late.at[way, other], late_sem.at[s.n, way, other], to))

    def send_joined(s):
        for way, to in ((0, s.plus), (1, s.minus)):
            buf = s.early.at[way]
            remote(buf, buf, early_sem.at[s.n, way], twin).wait_recv()
            mine = s.at(s.full, 1 if way == 0 else 3, way * s.half, s.half)
            buf[...] = (mine[...].astype(F32) + buf[...].astype(F32)).astype(BF)
            start(remote(buf, s.late.at[way, way], late_sem.at[s.n, way, way], to))

    def total(s, which):
        for way in range(2):
            buf = s.late.at[way, which]
            remote(buf, buf, late_sem.at[s.n, way, which], twin).wait_recv()
        return (
            s.at(s.full, 0, which * s.half, s.half)[...].astype(F32)
            + s.late.at[0, which][...].astype(F32)
            + s.late.at[1, which][...].astype(F32)
        )

    def join_q(step):
        buf = y_q.at[step]
        remote(buf, buf, yq_sem.at[step], twin).wait_recv()
        mine = whole(q0, g_one, step)
        mine[...] = (mine[...].astype(F32) + buf[...].astype(F32)).astype(BF)

    def join_core(s, j, step):
        buf = core_in.at[step, j]
        remote(buf, buf, core_two_sem.at[step, j], twin).wait_recv()
        mine = whole(s, g_two, step)
        mine[...] = (mine[...].astype(F32) + buf[...].astype(F32)).astype(BF)

    def unit_one(step):
        last_update(x_t, inn, one, g_one, share_one, (z + step) % 4 * 512)
        start(remote(whole(q1, g_one, step), y_q.at[step], yq_sem.at[step], q1.partner))

    def unit_two(step):
        last_update(h_t, err, two, g_two, share_two, (xx + step) % 4 * 512)
        for j, s in ((1, u1), (0, u0)):
            start(remote(whole(s, g_two, step), core_in.at[step, j], core_two_sem.at[step, j], twin))

    def to_pair(s, out, pair, n):
        for which in range(2):
            out[which * s.half : (which + 1) * s.half] = total(s, which).astype(BF)
        start(remote(out, pair, pair_sem.at[n], s.partner))

    out_t, out_p = y.at[pl.ds(0, 128)], x.at[pl.ds(0, P_ROWS)]
    def joins(step):
        for j, s in ((1, t1), (0, t0)):
            join_core(s, j, step)

    unit_one(2)
    send_early(p1)
    unit_one(1)
    send_plain(p1, 0)
    unit_one(3)
    send_plain(p1, 1)
    send_early(p0)
    unit_two(2)
    send_joined(p1)
    send_plain(p0, 0)
    send_plain(p0, 1)
    unit_two(1)
    joins(2)
    send_early(t1)
    send_early(t0)
    join_q(2)
    send_early(q0)
    unit_one(0)
    joins(1)
    send_plain(t1, 0)
    send_plain(t0, 0)
    join_q(1)
    send_plain(q0, 0)
    unit_two(3)
    send_joined(p0)
    join_q(3)
    send_plain(q0, 1)
    unit_two(0)
    joins(3)
    send_plain(t1, 1)
    send_joined(t1)
    send_plain(t0, 1)
    send_joined(t0)
    to_pair(p1, out_p, pair_p, 0)
    joins(0)
    join_q(0)
    send_joined(q0)
    to_pair(t1, out_t, pair_t, 1)
    for which in range(2):
        first = P_ROWS + which * q0.half
        slope[first : first + q0.half] = total(q0, which)
    done = pltpu.make_async_copy(slope.at[pl.ds(0, 128)], avg_two, local_sem.at[5])
    for s, out, pair, n in ((t0, out_t, pair_t, 1), (p0, out_p, pair_p, 0)):
        full = [total(s, which) for which in range(2)]
        remote(out, pair, pair_sem.at[n], twin).wait_recv()
        if n == 0:
            done.wait()
        for which in range(2):
            rows = slice(which * s.half, (which + 1) * s.half)
            slope[rows] = full[which] + pair[rows].astype(F32)
        if n == 1:
            done.start()
    done = pltpu.make_async_copy(slope, avg_one, local_sem.at[5])
    done.start()
    for copy in sent:
        copy.wait_send()
    done.wait()


def one_round(routes, counts, docs, targs, module_one, module_two):
    sem = pltpu.SemaphoreType.DMA
    v = lambda *shape: pltpu.VMEM(shape, BF)
    act = v(SLOTS, D)
    p, q = P_ROWS // 2, Q_ROWS // 2
    return pl.pallas_call(
        round_kernel,
        out_shape=(
            jax.ShapeDtypeStruct((4, PATHS, 8, D // 4), BF),
            jax.ShapeDtypeStruct((4, PATHS * 8, D // 4), BF),
            jax.ShapeDtypeStruct((256, D), F32),
            jax.ShapeDtypeStruct((128, D), F32),
        ),
        in_specs=[VMEM] + [ANY] * 5,
        out_specs=(ANY, ANY, ANY, ANY),
        scratch_shapes=[pltpu.VMEM((N_COL, N_ROW), jnp.int32)]
        + [v(D, D)] * 4
        + [v(4, 32, 8, D // 4)]
        + [act] * 5
        + [pltpu.VMEM((SLOTS, D), F32)]
        + [v(D, SLOTS)] * 2
        + [v(2, 2, p, D), v(2, 2, 2, p, D), v(2 * p, D)]
        + [v(4, 2 * q, D), v(2, q, D), v(2, 2, q, D)]
        + [v(4, 2, 128, D), v(2, 2, 64, D), v(2, 2, 2, 64, D), v(128, D)]
        + [sem((5, 2, 2, 2)), sem((5, 2, 2)), sem((2, 2)), sem((4, 2)), sem((4, 2, 2)), sem((4, 2)), sem((8,))]
        + [sem((5, 2, 2)), sem((5, 2, 2, 2)), sem((2, 2)), sem((4, 2)), sem((4, 2, 2)), sem((4,)), sem((4,))],
        compiler_params=pltpu.CompilerParams(has_side_effects=True, collective_id=0, vmem_limit_bytes=67043328),
        name="round",
    )(routes, counts, docs, targs, module_one, module_two)


def shards(documents, targets, routes, doc_counts, module_one, module_two, moment_one, moment_two):
    got, packed, avg_one, avg_two = one_round(
        routes.reshape(2, 1, ROWS), doc_counts.T, documents, targets, module_one, module_two
    )
    next_moment_one = outer_moment * moment_one + avg_one[None]
    next_moment_two = outer_moment * moment_two + avg_two[None]
    new_one = module_one - outer_rate * (outer_moment * next_moment_one + avg_one[None])
    new_two = module_two - outer_rate * (outer_moment * next_moment_two + avg_two[None])
    return (new_one, new_two, next_moment_one, next_moment_two)


def solution(mesh):
    return jax.shard_map(
        shards,
        mesh=mesh,
        in_specs=(
            P(None, ("row", "col"), None),
            P(None, ("row", "col"), None),
            P(None, ("row", "col"), None),
            P(),
            P("row", "col", None),
            P("col", "row", None),
            P("row", "col", None),
            P("col", "row", None),
        ),
        out_specs=(
            P("row", "col", None),
            P("col", "row", None),
            P("row", "col", None),
            P("col", "row", None),
        ),
        check_vma=False,
    )
```

```python
import functools

import jax
import jax.numpy as jnp
from jax import lax
from jax.experimental import pallas as pl
from jax.experimental.pallas import tpu as pltpu
from jax.sharding import PartitionSpec as P

D = 2048
ROWS = 128
PATHS = 128
SLOTS = 256
N_ROW = 16
N_COL = 8
SCALE = D ** (-0.5)
GUARD = 0.5 / (D * ROWS) ** 0.5 / SCALE

outer_rate = 0.7
outer_moment = 0.9

BF = jnp.bfloat16
F32 = jnp.float32
MESH = pl.DeviceIdType.MESH
ANY = pl.BlockSpec(memory_space=pl.ANY)
VMEM = pl.BlockSpec(memory_space=pltpu.VMEM)


def iota(shape, dim):
    return lax.broadcasted_iota(jnp.int32, shape, dim)


P_GATHER = 160
P_ROWS = 160
Q_ROWS = 256 - P_ROWS


class Stream:
    def __init__(self, **fields):
        self.__dict__.update(fields)

    def at(self, full, step, first, count):
        return full.at[pl.ds(pl.multiple_of(self.rows((self.place + step) % 4) + first, 8), count)]


def remote(src, dst, sems, device):
    return pltpu.make_async_remote_copy(
        src_ref=src, dst_ref=dst, send_sem=sems.at[0], recv_sem=sems.at[1], device_id=device, device_id_type=MESH
    )


def round_kernel(
    routes, counts_in, docs, targs, module_one, module_two, got, packed, avg_one, avg_two,
    counts,
    one, two, g_one, g_two, stage, x, y, hid, err, inn, slope, x_t, h_t,
    early_p, late_p, pair_p, y_q, early_q, late_q, core_in, early_t, late_t, pair_t,
    ring_sem, fwd_sem, y_sem, q_sem, core_sem, a2a_sem, local_sem,
    early_sem, late_sem, pair_sem, yq_sem, core_two_sem, pack_sem, own_sem,
):
    row, col = lax.axis_index("row"), lax.axis_index("col")
    xx, low, core = row // 4, (row // 2) % 2, row % 2
    z, high = col // 2, col % 2
    me = row * N_COL + col

    def device(x=xx, low=low, core=core, z=z, high=high):
        return (x * 4 + low * 2 + core, z * 2 + high)

    twin = device(core=1 - core)
    ring_one = dict(place=z, plus=device(z=(z + 1) % 4), minus=device(z=(z + 3) % 4), partner=device(high=1 - high))
    ring_two = dict(place=xx, plus=device(x=(xx + 1) % 4), minus=device(x=(xx + 3) % 4), partner=device(low=1 - low))

    def rows_one(first, j):
        return lambda place: (place * 2 + (high + j) % 2) * 256 + first

    def rows_two(j, core=core):
        return lambda place: (place * 4 + ((low + j) % 2) * 2 + core) * 128

    def parts_one(rows):
        p = [Stream(n=j, half=rows // 2, rows=rows_one(0, j), **ring_one) for j in range(2)]
        q = [Stream(n=2, half=128 - rows // 2, rows=rows_one(rows, j), **ring_one) for j in range(2)]
        return p + q

    p0, p1, q0, q1 = parts_one(P_GATHER)
    t0 = Stream(n=3, half=64, rows=rows_two(0), **ring_two)
    t1 = Stream(n=4, half=64, rows=rows_two(1), **ring_two)
    u0 = Stream(half=64, rows=rows_two(0, 1 - core), **ring_two)
    u1 = Stream(half=64, rows=rows_two(1, 1 - core), **ring_two)
    sent = []

    def start(copy):
        copy.start()
        sent.append(copy)

    def whole(s, full, step):
        return s.at(full, step, 0, 2 * s.half)

    def spread(s, full):
        for way, to in ((0, s.plus), (1, s.minus)):
            for which in (0, 1) if way == 0 else (1, 0):
                ref = s.at(full, 0, which * s.half, s.half)
                start(remote(ref, ref, ring_sem.at[s.n, way, which], to))

    def arrived(s, full, way, which):
        ref = s.at(full, 3 if way == 0 else 1, which * s.half, s.half)
        remote(ref, ref, ring_sem.at[s.n, way, which], twin).wait_recv()

    def forward(s, full):
        for way, to in ((0, s.plus), (1, s.minus)):
            arrived(s, full, way, way)
            ref = s.at(full, 3 if way == 0 else 1, way * s.half, s.half)
            start(remote(ref, ref, fwd_sem.at[s.n, way], to))

    def rest(s, full):
        arrived(s, full, 0, 1)
        arrived(s, full, 1, 0)

    def forwarded(s, full):
        for way in range(2):
            ref = s.at(full, 2, way * s.half, s.half)
            remote(ref, ref, fwd_sem.at[s.n, way], twin).wait_recv()

    def q_across(step):
        ref = whole(q0, one, step)
        start(remote(ref, ref, q_sem.at[step], q0.partner))

    def to_twin(s, j, step):
        ref = whole(s, two, step)
        start(remote(ref, ref, core_sem.at[step, j], twin))

    def unpack(ch, into):
        o, i = iota((256, 256), 0), iota((256, 256), 1)
        source = o % 64 // 2 * 8 + o % 2 * 4 + o // 64
        pick = jnp.where(i == source, 1.0, 0.0).astype(BF)
        loads = [
            pltpu.make_async_copy(got.at[ch, pl.ds(b * 32, 32)], stage.at[b], local_sem.at[b]) for b in range(4)
        ]
        for copy in loads:
            copy.start()
        for b in range(4):
            loads[b].wait()
            rows = jnp.dot(pick, stage[b].reshape(256, 512), preferred_element_type=F32).astype(BF)
            for quarter in range(4):
                cols = slice(quarter * 512, (quarter + 1) * 512)
                into[b * 64 : (b + 1) * 64, cols] = rows[quarter * 64 : (quarter + 1) * 64]

    barrier = pltpu.get_barrier_semaphore()

    def greet(step, carry):
        for n in range(8):
            to = device(
                x=(xx + n % 4) % 4,
                low=(low + n // 4) % 2,
                high=(high + step % 2) % 2,
                z=(z + step // 2 % 4) % 4,
                core=(core + step // 8) % 2,
            )
            pl.semaphore_signal(barrier, inc=1, device_id=to, device_id_type=MESH)
        return carry

    upper = pltpu.make_async_copy(module_one.at[0, pl.ds(0, 128)], slope.at[pl.ds(0, 128)], local_sem.at[0])
    lower = pltpu.make_async_copy(module_one.at[0, pl.ds(128, 128)], slope.at[pl.ds(0, 128)], local_sem.at[1])
    other = pltpu.make_async_copy(module_two.at[0], slope.at[pl.ds(128, 128)], local_sem.at[2])
    upper.start()
    other.start()
    loads = [
        pltpu.make_async_copy(source.at[m], to.at[pl.ds(m * ROWS, ROWS)], local_sem.at[3 + m * 2 + n])
        for m in range(2)
        for n, (source, to) in enumerate(((docs, x), (targs, y)))
    ]
    loads.append(pltpu.make_async_copy(counts_in, counts, local_sem.at[7]))
    for copy in loads:
        copy.start()
    for n in range(1, 8):
        to = device(x=(xx + n % 4) % 4, low=(low + n // 4) % 2)
        pl.semaphore_signal(barrier, inc=1, device_id=to, device_id_type=MESH)
    lax.fori_loop(1, 16, greet, 0)
    upper.wait()
    p0.at(one, 0, 0, 128)[...] = slope[0:128].astype(BF)
    lower.start()
    other.wait()
    whole(t0, two, 0)[...] = slope[128:256].astype(BF)
    lower.wait()
    p0.at(one, 0, 128, 128)[...] = slope[0:128].astype(BF)
    pl.semaphore_wait(barrier, PATHS - 1)
    start(remote(whole(p0, one, 0), whole(p0, one, 0), y_sem.at[0], p0.partner))
    start(remote(whole(t0, two, 0), whole(t0, two, 0), y_sem.at[1], t0.partner))
    spread(p0, one)
    spread(t0, two)
    spread(q0, one)
    q_across(0)
    to_twin(t0, 0, 0)
    for copy in loads:
        copy.wait()

    def pack(m):
        to = routes[m]
        same_place = iota((ROWS, ROWS), 0) == iota((ROWS, ROWS), 1)
        down = jnp.sum(jnp.where(same_place, to, 0), axis=1, keepdims=True)
        same = jnp.where(down == to, 1, 0)
        earlier = jnp.where(iota((ROWS, ROWS), 0) < iota((ROWS, ROWS), 1), same, 0)
        rank = jnp.sum(earlier, axis=0, keepdims=True)

        def block(b, carry):
            for kind, source in enumerate((x, y)):
                total = jnp.zeros((256, 512), F32)
                for quarter in range(4):
                    slot = to * 8 + rank * 4 + quarter - b * 256
                    pick = jnp.where(iota((256, ROWS), 0) == slot, 1.0, 0.0).astype(BF)
                    part = source[m * ROWS : (m + 1) * ROWS, quarter * 512 : (quarter + 1) * 512]
                    total += jnp.dot(pick, part, preferred_element_type=F32)
                rows = pl.ds(pl.multiple_of(b * 256, 256), 256)
                g_one[rows, (m * 2 + kind) * 512 : (m * 2 + kind + 1) * 512] = total.astype(BF)
            return carry

        lax.fori_loop(0, 4, block, 0)
        for kind in range(2):
            pltpu.make_async_copy(packed_part(m * 2 + kind), packed.at[m * 2 + kind], pack_sem.at[m * 2 + kind]).start()
        for kind in range(2):
            pltpu.make_async_copy(packed_part(m * 2 + kind), packed.at[m * 2 + kind], pack_sem.at[m * 2 + kind]).wait()

    def packed_part(ch):
        return g_one.at[pl.ds(0, PATHS * 8), pl.ds(ch * 512, 512)]

    def slot_rows(m, path):
        return packed.at[m, pl.ds(pl.multiple_of(path * 8, 8), 8)]

    row_of = [(xx + n % 4) % 4 * 4 + (low + n // 4) % 2 * 2 for n in range(8)]

    def send_slots(m):
        def send(turn, n):
            t = n * 85 % PATHS
            u = lax.rem(turn * 5 + t // 8, 16)
            to_high = lax.rem(high + lax.rem(u, 2), 2)
            to_z = lax.rem(z + lax.rem(lax.div(u, 2), 4), 4)
            to_core = lax.rem(core + lax.div(u, 8), 2)
            to = (row_of[t % 8] + to_core, to_z * 2 + to_high)
            remote(slot_rows(m, to[0] * N_COL + to[1]), got.at[m, me], a2a_sem.at[m], to).start()

        def eight(turn, carry):
            for n in range(8):
                send(turn, n)
            return carry

        for n in range(1, 8):
            send(jnp.int32(0), n)
        lax.fori_loop(1, 16, eight, 0)

    def all_slots(m):
        ref = got.at[m, pl.ds(0, PATHS - 1)]
        return remote(ref, ref, a2a_sem.at[m], twin)

    own_slots = [pltpu.make_async_copy(slot_rows(ch, me), got.at[ch, me], own_sem.at[ch]) for ch in range(4)]
    for m in range(2):
        pack(m)
        for kind in range(2):
            own_slots[m * 2 + kind].start()
            if m == 0:
                send_slots(kind)
    remote(whole(p1, one, 0), whole(p1, one, 0), y_sem.at[0], twin).wait_recv()
    spread(p1, one)
    remote(whole(t1, two, 0), whole(t1, two, 0), y_sem.at[1], twin).wait_recv()
    spread(t1, two)
    to_twin(t1, 1, 0)
    forward(p0, one)
    forward(t0, two)
    forward(q0, one)
    forward(p1, one)
    forward(t1, two)
    rest(q0, one)
    q_across(1)
    q_across(3)
    for j, s in ((0, t0), (1, t1)):
        rest(s, two)
        to_twin(s, j, 1)
        to_twin(s, j, 3)
    forwarded(q0, one)
    q_across(2)
    for j, s in ((0, t0), (1, t1)):
        forwarded(s, two)
        to_twin(s, j, 2)
    for copy in own_slots:
        copy.wait()
    all_slots(0).wait_recv()
    unpack(0, x)
    all_slots(1).wait_recv()
    unpack(1, y)
    for step in range(4):
        ref = whole(q1, one, step)
        remote(ref, ref, q_sem.at[step], twin).wait_recv()
        for j, s in ((0, u0), (1, u1)):
            ref = whole(s, two, step)
            remote(ref, ref, core_sem.at[step, j], twin).wait_recv()
    for s in (p0, p1):
        rest(s, one)
        forwarded(s, one)
    send_slots(2)

    def spans(n, tile):
        return pl.ds(pl.multiple_of(n * tile, tile), tile)

    wide = 1024

    def pre_pass():
        def pre_tile(n, carry):
            cols = spans(n, wide)
            pre = jnp.dot(x[...], one[:, cols], preferred_element_type=F32) * SCALE
            sig = 1.0 / (1.0 + jnp.exp(-pre))
            hid[:, cols] = (pre * sig).astype(BF)
            slope[:, cols] = sig * (1.0 + pre * (1.0 - sig))
            return carry

        lax.fori_loop(0, D // wide, pre_tile, 0)

    def err_pass():
        def err_tile(n, carry):
            cols = spans(n, wide)
            out = jnp.dot(hid[...], two[:, cols], preferred_element_type=F32) * SCALE
            out = x[:, cols].astype(F32) + out
            err[:, cols] = ((out - y[:, cols].astype(F32)) / ROWS).astype(BF)
            return carry

        lax.fori_loop(0, D // wide, err_tile, 0)

        def inn_tile(n, carry):
            cols = spans(n, wide)
            back = lax.dot_general(err[...], two[cols, :], (((1,), (1,)), ((), ())), preferred_element_type=F32)
            inn[:, cols] = (back * SCALE * slope[:, cols]).astype(BF)
            return carry

        lax.fori_loop(0, D // wide, inn_tile, 0)

    def turns():
        def turn(n, carry):
            cols = spans(n, 256)
            x_t[cols, :] = x[:, cols].T
            h_t[cols, :] = hid[:, cols].T
            return carry

        lax.fori_loop(0, D // 256, turn, 0)

    def first_update(left, right, w, g):
        def step(n, carry):
            rows, cols = spans(n // 4, 1024), spans(n % 4, 512)
            grad = jnp.dot(left[rows, :], right[:, cols], preferred_element_type=F32)
            update = grad / (jnp.abs(grad) + GUARD)
            g[rows, cols] = grad.astype(BF)
            w[rows, cols] = (0.99 * w[rows, cols].astype(F32) - 0.1 * update).astype(BF)
            return carry

        lax.fori_loop(0, 8, step, 0)

    tally = counts[...].astype(F32)
    in_row = jnp.where(iota((N_COL, N_ROW), 1) == row, tally, 0.0)
    in_col = jnp.where(iota((N_COL, N_ROW), 0) == col, tally, 0.0)
    mine = jnp.where(iota((N_COL, N_ROW), 0) == col, in_row, 0.0)

    def grand(v):
        return jnp.sum(jnp.sum(v, axis=0, keepdims=True), axis=1, keepdims=True)

    share_one, share_two = grand(mine) / grand(in_row), grand(mine) / grand(in_col)
    root = (0.05 / 0.0975) ** 0.5

    def last_update(left, right, w, g, weight, first_row):
        part_w, part_a = weight * (1.0 / 0.99 - 0.99), weight * (0.1 / 0.99)
        part_b = weight * (0.1 * (0.1 / 0.19) / root)

        def step(n, carry):
            rows, cols = pl.ds(pl.multiple_of(first_row, 512), 512), spans(n, 512)
            grad = jnp.dot(left[rows, :], right[:, cols], preferred_element_type=F32)
            before = g[rows, cols].astype(F32)
            update_a = before / (jnp.abs(before) + GUARD)
            second = 0.95 * (before * before) + grad * grad
            update_b = (0.9 * before + grad) / (jnp.sqrt(second) + GUARD / root)
            g[rows, cols] = (
                part_w * w[rows, cols].astype(F32) + part_a * update_a + part_b * update_b
            ).astype(BF)
            return carry

        lax.fori_loop(0, 4, step, 0)

    pre_pass()
    err_pass()
    turns()
    send_slots(3)
    for copy in sent:
        copy.wait_send()
    sent.clear()
    first_update(x_t, inn, one, g_one)
    all_slots(2).wait_recv()
    unpack(2, x)
    pre_pass()
    first_update(h_t, err, two, g_two)
    turns()
    all_slots(3).wait_recv()
    unpack(3, y)
    err_pass()
    for ch in range(4):
        all_slots(ch).wait_send()

    p0, p1, q0, q1 = parts_one(P_ROWS)
    for s, full, early, late in (
        (p0, g_one, early_p.at[0], late_p.at[0]),
        (p1, g_one, early_p.at[1], late_p.at[1]),
        (q0, g_one, early_q, late_q),
        (t0, g_two, early_t.at[0], late_t.at[0]),
        (t1, g_two, early_t.at[1], late_t.at[1]),
    ):
        s.full, s.early, s.late = full, early, late

    def send_early(s):
        for way, to in ((0, s.plus), (1, s.minus)):
            src = s.at(s.full, 2, way * s.half, s.half)
            start(remote(src, s.early.at[way], early_sem.at[s.n, way], to))

    def send_plain(s, way):
        other = 1 - way
        src = s.at(s.full, 1 if way == 0 else 3, other * s.half, s.half)
        to = s.plus if way == 0 else s.minus
        start(remote(src, s.late.at[way, other], late_sem.at[s.n, way, other], to))

    def send_joined(s):
        for way, to in ((0, s.plus), (1, s.minus)):
            buf = s.early.at[way]
            remote(buf, buf, early_sem.at[s.n, way], twin).wait_recv()
            mine = s.at(s.full, 1 if way == 0 else 3, way * s.half, s.half)
            buf[...] = (mine[...].astype(F32) + buf[...].astype(F32)).astype(BF)
            start(remote(buf, s.late.at[way, way], late_sem.at[s.n, way, way], to))

    def total(s, which):
        for way in range(2):
            buf = s.late.at[way, which]
            remote(buf, buf, late_sem.at[s.n, way, which], twin).wait_recv()
        return (
            s.at(s.full, 0, which * s.half, s.half)[...].astype(F32)
            + s.late.at[0, which][...].astype(F32)
            + s.late.at[1, which][...].astype(F32)
        )

    def join_q(step):
        buf = y_q.at[step]
        remote(buf, buf, yq_sem.at[step], twin).wait_recv()
        mine = whole(q0, g_one, step)
        mine[...] = (mine[...].astype(F32) + buf[...].astype(F32)).astype(BF)

    def join_core(s, j, step):
        buf = core_in.at[step, j]
        remote(buf, buf, core_two_sem.at[step, j], twin).wait_recv()
        mine = whole(s, g_two, step)
        mine[...] = (mine[...].astype(F32) + buf[...].astype(F32)).astype(BF)

    def unit_one(step):
        last_update(x_t, inn, one, g_one, share_one, (z + step) % 4 * 512)
        start(remote(whole(q1, g_one, step), y_q.at[step], yq_sem.at[step], q1.partner))

    def unit_two(step):
        last_update(h_t, err, two, g_two, share_two, (xx + step) % 4 * 512)
        for j, s in ((1, u1), (0, u0)):
            start(remote(whole(s, g_two, step), core_in.at[step, j], core_two_sem.at[step, j], twin))

    def to_pair(s, out, pair, n):
        for which in range(2):
            out[which * s.half : (which + 1) * s.half] = total(s, which).astype(BF)
        start(remote(out, pair, pair_sem.at[n], s.partner))

    out_t, out_p = y.at[pl.ds(0, 128)], x.at[pl.ds(0, P_ROWS)]
    def joins(step):
        for j, s in ((1, t1), (0, t0)):
            join_core(s, j, step)

    unit_one(2)
    send_early(p1)
    unit_one(1)
    send_plain(p1, 0)
    unit_one(3)
    send_plain(p1, 1)
    send_early(p0)
    unit_two(2)
    send_joined(p1)
    send_plain(p0, 0)
    send_plain(p0, 1)
    unit_two(1)
    joins(2)
    send_early(t1)
    send_early(t0)
    join_q(2)
    send_early(q0)
    unit_one(0)
    joins(1)
    send_plain(t1, 0)
    send_plain(t0, 0)
    join_q(1)
    send_plain(q0, 0)
    unit_two(3)
    send_joined(p0)
    join_q(3)
    send_plain(q0, 1)
    unit_two(0)
    joins(3)
    send_plain(t1, 1)
    send_joined(t1)
    send_plain(t0, 1)
    send_joined(t0)
    to_pair(p1, out_p, pair_p, 0)
    joins(0)
    join_q(0)
    send_joined(q0)
    to_pair(t1, out_t, pair_t, 1)
    for which in range(2):
        first = P_ROWS + which * q0.half
        slope[first : first + q0.half] = total(q0, which)
    done = pltpu.make_async_copy(slope.at[pl.ds(0, 128)], avg_two, local_sem.at[5])
    for s, out, pair, n in ((t0, out_t, pair_t, 1), (p0, out_p, pair_p, 0)):
        full = [total(s, which) for which in range(2)]
        remote(out, pair, pair_sem.at[n], twin).wait_recv()
        if n == 0:
            done.wait()
        for which in range(2):
            rows = slice(which * s.half, (which + 1) * s.half)
            slope[rows] = full[which] + pair[rows].astype(F32)
        if n == 1:
            done.start()
    done = pltpu.make_async_copy(slope, avg_one, local_sem.at[5])
    done.start()
    for copy in sent:
        copy.wait_send()
    done.wait()


def one_round(routes, counts, docs, targs, module_one, module_two):
    sem = pltpu.SemaphoreType.DMA
    v = lambda *shape: pltpu.VMEM(shape, BF)
    act = v(SLOTS, D)
    p, q = P_ROWS // 2, Q_ROWS // 2
    return pl.pallas_call(
        round_kernel,
        out_shape=(
            jax.ShapeDtypeStruct((4, PATHS, 8, D // 4), BF),
            jax.ShapeDtypeStruct((4, PATHS * 8, D // 4), BF),
            jax.ShapeDtypeStruct((256, D), F32),
            jax.ShapeDtypeStruct((128, D), F32),
        ),
        in_specs=[VMEM] + [ANY] * 5,
        out_specs=(ANY, ANY, ANY, ANY),
        scratch_shapes=[pltpu.VMEM((N_COL, N_ROW), jnp.int32)]
        + [v(D, D)] * 4
        + [v(4, 32, 8, D // 4)]
        + [act] * 5
        + [pltpu.VMEM((SLOTS, D), F32)]
        + [v(D, SLOTS)] * 2
        + [v(2, 2, p, D), v(2, 2, 2, p, D), v(2 * p, D)]
        + [v(4, 2 * q, D), v(2, q, D), v(2, 2, q, D)]
        + [v(4, 2, 128, D), v(2, 2, 64, D), v(2, 2, 2, 64, D), v(128, D)]
        + [sem((5, 2, 2, 2)), sem((5, 2, 2)), sem((2, 2)), sem((4, 2)), sem((4, 2, 2)), sem((4, 2)), sem((8,))]
        + [sem((5, 2, 2)), sem((5, 2, 2, 2)), sem((2, 2)), sem((4, 2)), sem((4, 2, 2)), sem((4,)), sem((4,))],
        compiler_params=pltpu.CompilerParams(has_side_effects=True, collective_id=0, vmem_limit_bytes=67043328),
        name="round",
    )(routes, counts, docs, targs, module_one, module_two)


def shards(documents, targets, routes, doc_counts, module_one, module_two, moment_one, moment_two):
    got, packed, avg_one, avg_two = one_round(
        routes.reshape(2, 1, ROWS), doc_counts.T, documents, targets, module_one, module_two
    )
    next_moment_one = outer_moment * moment_one + avg_one[None]
    next_moment_two = outer_moment * moment_two + avg_two[None]
    new_one = module_one - outer_rate * (outer_moment * next_moment_one + avg_one[None])
    new_two = module_two - outer_rate * (outer_moment * next_moment_two + avg_two[None])
    return (new_one, new_two, next_moment_one, next_moment_two)


def solution(mesh):
    return jax.shard_map(
        shards,
        mesh=mesh,
        in_specs=(
            P(None, ("row", "col"), None),
            P(None, ("row", "col"), None),
            P(None, ("row", "col"), None),
            P(),
            P("row", "col", None),
            P("col", "row", None),
            P("row", "col", None),
            P("col", "row", None),
        ),
        out_specs=(
            P("row", "col", None),
            P("col", "row", None),
            P("row", "col", None),
            P("col", "row", None),
        ),
        check_vma=False,
    )
```
